512 devices in a mesh: row: 16 (over x, y), col: 32 (over z, core).
Axes of the slice: x: 4, y: 4, z: 16, core: 2. Of those that a mesh axis runs over, the one named last changes fastest.
Arguments:
- diag_block: float32 [512, 512], P('row', 'col'), as said below
- panel: float32 [14336, 512], P(('row', 'col')), may hold values from -0.625 to 0.625
- trailing: float32 [14336, 14336], P('row', 'col'), may hold values from -6 to 6
- truth_panel: float32 [5120, 512], P('row', 'col'), may hold values from -0.625 to 0.625
- truth_rest: float32 [5120, 14336], P('row', 'col'), may hold values from -6 to 6
Outputs:
- factor: float32 [14336, 512], P(('row', 'col'))
- updated: float32 [14336, 14336], P('row', 'col')
- solved: float32 [5120, 512], P('row', 'col')
- truth_updated: float32 [5120, 14336], P('row', 'col')
The draws below stay inside these ranges and needn't reach their ends.
Inputs may be any that keep to these rules, and one draw needn't show every extreme that they name: diag_block is symmetric positive definite.
All inputs are finite; a program needn't handle non-finite values.
Results may differ from the reference program's by a relative error of at most 0.00014.
Values sent between devices are 32-bit elements; how exact they have to be, the bound alone decides.
No kernel may reach another device: no remote copies, remote signals or barrier semaphores. Data moves between devices by JAX's collectives and lax.ppermute only.
A program may use at most 64 MiB of HBM per device.

```python
import jax
import jax.numpy as jnp
from jax import lax

PANEL = 512
ORDER = 14336
TRUTH = 5120
N_ROW = 16
N_COL = 32
DEVICES = 512


def draw_diag_block(key, part):
    first = jax.random.fold_in(key, 11)
    second = jax.random.fold_in(key, 12)
    random_part = jax.random.normal(first, (PANEL, PANEL), jnp.float32)
    gram = jnp.dot(random_part, random_part.T, precision=lax.Precision.HIGHEST) / PANEL
    extra = jnp.exp(jax.random.uniform(second, (PANEL,), jnp.float32, jnp.log(0.5), jnp.log(2.0)))
    matrix = gram + jnp.diag(extra)
    return 0.5 * (matrix + matrix.T)


def shard_levels(stream_key, extent, cuts, least, top_value):
    def one(dim, shards_of):
        heights = jax.random.uniform(jax.random.fold_in(jax.random.fold_in(stream_key, 6), dim), (shards_of,), jnp.float32, least / len(cuts), top_value / len(cuts))
        return jnp.repeat(jnp.exp(heights), extent[dim] // shards_of).reshape((-1,) + (1,) * (len(extent) - dim - 1))

    loudness = one(*cuts[0])
    for cut in cuts[1:]:
        loudness = loudness * one(*cut)
    return loudness


def centred(key, extent, scale, bound, shards=(), held_as=jnp.bfloat16):
    values = scale * jax.random.normal(key, extent, jnp.float32)
    if shards:
        values = values * shard_levels(key, extent, shards, -0.22, 0.18)
    return jnp.clip(values, -bound, bound).astype(held_as)


def setup_inputs(seed: int = 0) -> dict:
    arg_keys = jax.random.split(jax.random.key(seed), 6)
    diag_block = draw_diag_block(jax.random.fold_in(arg_keys[5], 71), 0)
    panel = centred(arg_keys[1], (ORDER, PANEL), (PANEL ** -0.5), 0.625, ((0, 512),), jnp.float32)
    trailing = centred(arg_keys[2], (ORDER, ORDER), 1.0, 6.0, ((0, 16), (1, 32)), jnp.float32)
    truth_panel = centred(arg_keys[3], (TRUTH, PANEL), (PANEL ** -0.5), 0.625, ((0, 16), (1, 32)), jnp.float32)
    truth_rest = centred(arg_keys[4], (TRUTH, ORDER), 1.0, 6.0, ((0, 16), (1, 32)), jnp.float32)
    return dict(diag_block=diag_block, panel=panel, trailing=trailing, truth_panel=truth_panel, truth_rest=truth_rest)


precise = lax.Precision.HIGHEST

def right_solve(lower_factor, right_side):
    return jax.scipy.linalg.solve_triangular(lower_factor, right_side.T, lower=True).T

def reference(diag_block, panel, trailing, truth_panel, truth_rest):
    lower_factor = jnp.linalg.cholesky(diag_block)
    factor = right_solve(lower_factor, panel)
    tile_rows = ORDER // DEVICES
    dealt_rows = factor.reshape(N_ROW, N_COL, tile_rows, PANEL).transpose(1, 0, 2, 3).reshape(ORDER, PANEL)
    updated = trailing - jnp.dot(factor, dealt_rows.T, precision=precise)
    solved = right_solve(lower_factor, truth_panel)
    truth_updated = truth_rest - jnp.dot(solved, dealt_rows.T, precision=precise)
    return (factor, updated, solved, truth_updated)
```

```python
import jax
import jax.numpy as jnp
from jax import lax
from jax.experimental import pallas as pl
from jax.experimental.pallas import tpu as pltpu
from jax.sharding import PartitionSpec as P
HI = lax.Precision.HIGHEST
NT = (((1,), (1,)), ((), ()))
NN = (((1,), (0,)), ((), ()))

def factor_tile(d_ref, o_ref):
    n = 16
    lane = lax.broadcasted_iota(jnp.int32, (8, 128), 1)
    sub = lax.broadcasted_iota(jnp.int32, (8, 128), 0)
    full = lambda v: jnp.broadcast_to(v, (8, 128))
    m = [d_ref[8 * i:8 * i + 8, :] for i in range(n)]
    for j in range(n):
        lo = 8 * j
        here = (lane >= lo) & (lane < lo + 8)
        own = m[j]
        cols = [full(own[:, lo + c:lo + c + 1]) for c in range(8)]
        s = {(a, c): full(cols[c][a:a + 1, :]) for c in range(8) for a in range(c, 8)}
        rows = jnp.where(here, jnp.where(lane - lo == sub, 1.0, 0.0), own)
        r = [full(rows[a:a + 1, :]) for a in range(8)]
        l, inv, u = {}, [], []
        for c in range(8):
            q = lax.rsqrt(s[c, c])
            inv.append(q)
            for a in range(c + 1, 8):
                l[a, c] = s[a, c] * q
            for a in range(c + 1, 8):
                for b in range(c + 1, a + 1):
                    s[a, b] = s[a, b] - l[a, c] * l[b, c]
            u.append(r[c] * q)
            for a in range(c + 1, 8):
                r[a] = r[a] - l[a, c] * u[c]
        done = u[0]
        for a in range(1, 8):
            done = jnp.where(sub == a, u[a], done)
        o_ref[lo:lo + 8, :] = jnp.where(lane < lo + 8, done, 0.0)
        for i in range(j + 1, n):
            b = [full(m[i][:, lo + c:lo + c + 1]) for c in range(8)]
            acc = jnp.where(here, 0.0, m[i])
            for c in range(8):
                t = b[c] * inv[c]
                for e in range(c + 1, 8):
                    b[e] = b[e] - t * l[e, c]
                acc = acc - t * u[c]
            m[i] = acc

def chol_kernel(a_ref, o_ref, m_ref, d_ref, t_ref, u_ref):
    nb = 128
    n = a_ref.shape[0]
    m_ref[...] = a_ref[...]
    col = lax.broadcasted_iota(jnp.int32, (nb, n), 1)
    row = lax.broadcasted_iota(jnp.int32, (n, nb), 0)

    def step(k, _):
        at = pl.ds(pl.multiple_of(k * nb, nb), nb)
        d_ref[...] = m_ref[at, at]
        factor_tile(d_ref, t_ref)
        t = t_ref[...]
        left = lax.dot_general(m_ref[:, at], t, NT, precision=HI, preferred_element_type=jnp.float32)
        left = jnp.where(row >= (k + 1) * nb, left, 0.0)
        u_ref[...] = lax.dot_general(t, m_ref[at, :], NN, precision=HI, preferred_element_type=jnp.float32)
        u_ref[:, at] = t
        m_ref[:, at] = jnp.where(row >= (k + 1) * nb, 0.0, m_ref[:, at])
        m_ref[...] = m_ref[...] - lax.dot_general(left, u_ref[...], NN, precision=HI, preferred_element_type=jnp.float32)
        m_ref[at, :] = jnp.where(col < (k + 1) * nb, u_ref[...], 0.0)
        return 0
    lax.fori_loop(0, n // nb, step, 0)
    o_ref[...] = m_ref[...]


def invert_factor(block):
    n = block.shape[0]
    return pl.pallas_call(
        chol_kernel,
        out_shape=jax.ShapeDtypeStruct((n, n), jnp.float32),
        in_specs=[pl.BlockSpec(memory_space=pltpu.VMEM)],
        out_specs=pl.BlockSpec(memory_space=pltpu.VMEM),
        scratch_shapes=[
            pltpu.VMEM((n, n), jnp.float32),
            pltpu.VMEM((128, 128), jnp.float32),
            pltpu.VMEM((128, 128), jnp.float32),
            pltpu.VMEM((128, n), jnp.float32),
        ],
        cost_estimate=pl.CostEstimate(flops=10**10, bytes_accessed=2 * 10**6, transcendentals=0),
        name="invert_factor",
    )(block)


def spread(value, axes, count):
    copies = jnp.broadcast_to(value[None], (count,) + value.shape)
    return lax.all_to_all(copies, axes, 0, 0)


HIGH = lax.Precision.HIGH


def per_device(diag_block, panel, trailing, truth_panel, truth_rest):
    rows, columns = ("x", "y"), ("z", "k")
    packed = jnp.concatenate(
        [
            jnp.pad(panel, ((0, 4), (0, 0))),
            jnp.pad(truth_panel.T, ((0, 0), (0, 192))),
        ],
        0,
    )
    gathered = lax.all_gather(packed, columns, axis=0, tiled=False)
    pieces = spread(diag_block.reshape(4, 128), columns, 32)
    strip = pieces.reshape(32, 4, 8, 16).transpose(1, 2, 0, 3).reshape(32, 512)
    whole = spread(strip, rows, 16).reshape(512, 512)
    dealt = spread(panel, rows, 16).reshape(448, 512)
    inverse = invert_factor(whole)
    factor = lax.dot_general(panel, inverse, NT, precision=HI)
    dealt_rows = lax.dot_general(dealt, inverse, NT, precision=HIGH)
    own_rows = gathered[:, :28, :].reshape(896, 512)
    factor_rows = lax.dot_general(own_rows, inverse, NT, precision=HIGH)
    updated = trailing - lax.dot_general(factor_rows, dealt_rows, NT, precision=HIGH)
    truth_rows = gathered[:, 32:, :320].reshape(512, 320)
    solved_all = lax.dot_general(truth_rows, inverse, (((0,), (1,)), ((), ())), precision=HIGH)
    at = (lax.axis_index("z") * 2 + lax.axis_index("k")) * 16
    solved = lax.dynamic_slice_in_dim(solved_all, at, 16, 1)
    truth_updated = truth_rest - lax.dot_general(solved_all, dealt_rows, NT, precision=HIGH)
    return factor, updated, solved, truth_updated


def solution(mesh):
    fine = jax.sharding.Mesh(mesh.devices.reshape(4, 4, 16, 2), ("x", "y", "z", "k"))
    rows, columns = ("x", "y"), ("z", "k")
    tiled, whole = P(rows, columns), P(rows + columns, None)
    return jax.shard_map(
        per_device,
        mesh=fine,
        in_specs=(tiled, whole, tiled, tiled, tiled),
        out_specs=(whole, tiled, tiled, tiled),
        check_vma=False,
    )
```

```python
import jax
import jax.numpy as jnp
from jax import lax
from jax.experimental import pallas as pl
from jax.experimental.pallas import tpu as pltpu
from jax.sharding import PartitionSpec as P
HI = lax.Precision.HIGHEST
NT = (((1,), (1,)), ((), ()))
NN = (((1,), (0,)), ((), ()))

def factor_tile(d_ref, o_ref):
    n = 16
    lane = lax.broadcasted_iota(jnp.int32, (8, 128), 1)
    sub = lax.broadcasted_iota(jnp.int32, (8, 128), 0)
    full = lambda v: jnp.broadcast_to(v, (8, 128))
    m = [d_ref[8 * i:8 * i + 8, :] for i in range(n)]
    for j in range(n):
        lo = 8 * j
        here = (lane >= lo) & (lane < lo + 8)
        own = m[j]
        cols = [full(own[:, lo + c:lo + c + 1]) for c in range(8)]
        s = {(a, c): full(cols[c][a:a + 1, :]) for c in range(8) for a in range(c, 8)}
        rows = jnp.where(here, jnp.where(lane - lo == sub, 1.0, 0.0), own)
        r = [full(rows[a:a + 1, :]) for a in range(8)]
        l, inv, u = {}, [], []
        for c in range(8):
            q = lax.rsqrt(s[c, c])
            inv.append(q)
            for a in range(c + 1, 8):
                l[a, c] = s[a, c] * q
            for a in range(c + 1, 8):
                for b in range(c + 1, a + 1):
                    s[a, b] = s[a, b] - l[a, c] * l[b, c]
            u.append(r[c] * q)
            for a in range(c + 1, 8):
                r[a] = r[a] - l[a, c] * u[c]
        done = u[0]
        for a in range(1, 8):
            done = jnp.where(sub == a, u[a], done)
        o_ref[lo:lo + 8, :] = jnp.where(lane < lo + 8, done, 0.0)
        for i in range(j + 1, n):
            b = [full(m[i][:, lo + c:lo + c + 1]) for c in range(8)]
            acc = jnp.where(here, 0.0, m[i])
            for c in range(8):
                t = b[c] * inv[c]
                for e in range(c + 1, 8):
                    b[e] = b[e] - t * l[e, c]
                acc = acc - t * u[c]
            m[i] = acc

def chol_kernel(a_ref, o_ref, m_ref, d_ref, t_ref, u_ref):
    nb = 128
    n = a_ref.shape[0]
    m_ref[...] = a_ref[...]
    col = lax.broadcasted_iota(jnp.int32, (nb, n), 1)
    row = lax.broadcasted_iota(jnp.int32, (n, nb), 0)

    def step(k, _):
        at = pl.ds(pl.multiple_of(k * nb, nb), nb)
        d_ref[...] = m_ref[at, at]
        factor_tile(d_ref, t_ref)
        t = t_ref[...]
        left = lax.dot_general(m_ref[:, at], t, NT, precision=HI, preferred_element_type=jnp.float32)
        left = jnp.where(row >= (k + 1) * nb, left, 0.0)
        u_ref[...] = lax.dot_general(t, m_ref[at, :], NN, precision=HI, preferred_element_type=jnp.float32)
        u_ref[:, at] = t
        m_ref[:, at] = jnp.where(row >= (k + 1) * nb, 0.0, m_ref[:, at])
        m_ref[...] = m_ref[...] - lax.dot_general(left, u_ref[...], NN, precision=HI, preferred_element_type=jnp.float32)
        m_ref[at, :] = jnp.where(col < (k + 1) * nb, u_ref[...], 0.0)
        return 0
    lax.fori_loop(0, n // nb, step, 0)
    o_ref[...] = m_ref[...]


def invert_factor(block):
    n = block.shape[0]
    return pl.pallas_call(
        chol_kernel,
        out_shape=jax.ShapeDtypeStruct((n, n), jnp.float32),
        in_specs=[pl.BlockSpec(memory_space=pltpu.VMEM)],
        out_specs=pl.BlockSpec(memory_space=pltpu.VMEM),
        scratch_shapes=[
            pltpu.VMEM((n, n), jnp.float32),
            pltpu.VMEM((128, 128), jnp.float32),
            pltpu.VMEM((128, 128), jnp.float32),
            pltpu.VMEM((128, n), jnp.float32),
        ],
        cost_estimate=pl.CostEstimate(flops=10**10, bytes_accessed=2 * 10**6, transcendentals=0),
        name="invert_factor",
    )(block)


def spread(value, axes, count):
    copies = jnp.broadcast_to(value[None], (count,) + value.shape)
    return lax.all_to_all(copies, axes, 0, 0)


def halves(value):
    high = value.astype(jnp.bfloat16)
    return high, (value - high.astype(jnp.float32)).astype(jnp.bfloat16)


def thrice(a_high, a_low, b_high, b_low, dims):
    dot = lambda p, q: lax.dot_general(p, q, dims, preferred_element_type=jnp.float32)
    return dot(a_high, b_high) + dot(a_high, b_low) + dot(a_low, b_high)


def apply_kernel(
    col_ref, inv_hbm, dealt_hbm, gathered_hbm, panel_hbm, trailing_hbm, rest_hbm,
    factor_hbm, updated_hbm, solved_hbm, truth_hbm,
    inv, dealt, gathered, panel, trailing, rest,
    inv_high, inv_low, row_high, row_low, x_high, x_low, factor, solved, sem, out_sem,
):
    loads = [
        pltpu.make_async_copy(src, dst, sem.at[i])
        for i, (src, dst) in enumerate(
            [
                (inv_hbm, inv), (dealt_hbm, dealt), (gathered_hbm, gathered),
                (panel_hbm, panel), (trailing_hbm, trailing), (rest_hbm, rest),
            ]
        )
    ]
    for load in loads:
        load.start()
    loads[0].wait()
    inv_high[...], inv_low[...] = halves(inv[...])

    def solve(high, low):
        a = thrice(high[:, :256], low[:, :256], inv_high[:256, :256], inv_low[:256, :256], NT)
        b = thrice(high, low, inv_high[256:, :], inv_low[256:, :], NT)
        return jnp.concatenate([a, b], 1)

    loads[1].wait()
    for r in range(16):
        row_high[28 * r:28 * r + 28, :] = dealt[r]
    high, low = halves(row_high[...])
    done = solve(high, low)
    d_high, d_low = halves(done)
    loads[2].wait()
    loads[3].wait()
    stack = row_low
    for c in range(32):
        stack[28 * c:28 * c + 28, :] = gathered[c, 0:28, :]
    truth = gathered[:, 32:48, 0:384].reshape(512, 384)
    stack[896:1216, :] = truth.T[0:320, :]
    stack[1216:1244, :] = panel[...]
    stack[1244:1248, :] = jnp.zeros((4, 512), jnp.float32)
    at = pl.ds(pl.multiple_of(col_ref[0] * 16, 16), 16)
    i_high, i_low = halves(inv[at, :])
    t_high, t_low = halves(stack[896:1216, :])
    solved[...] = thrice(i_high, i_low, t_high, t_low, NT)
    for lo, hi in ((0, 416), (416, 832), (832, 1248)):
        high, low = halves(stack[lo:hi, :])
        part = solve(high, low)
        if hi == 1248:
            factor[...] = part[1216 - lo:1244 - lo, :]
        x_high[lo:hi, :], x_low[lo:hi, :] = halves(part)
    stores = [
        pltpu.make_async_copy(factor, factor_hbm, out_sem.at[0]),
        pltpu.make_async_copy(solved, solved_hbm, out_sem.at[1]),
    ]
    for store in stores:
        store.start()
    loads[4].wait()
    for i in range(4):
        a = slice(112 * i, 112 * i + 112)
        trailing[a, :] = trailing[a, :] - thrice(d_high[a], d_low[a], x_high[:896, :], x_low[:896, :], NT)
        store = pltpu.make_async_copy(trailing.at[a], updated_hbm.at[a], out_sem.at[2 + i])
        store.start()
        stores.append(store)
    loads[5].wait()
    rest[...] = rest[...] - thrice(x_high[896:1216, :], x_low[896:1216, :], d_high, d_low, NT)
    store = pltpu.make_async_copy(rest, truth_hbm, out_sem.at[6])
    store.start()
    stores.append(store)
    for store in stores:
        store.wait()


def apply_inverse(column, inverse, dealt, gathered, panel, trailing, rest):
    f32, bf16 = jnp.float32, jnp.bfloat16
    anywhere = pl.BlockSpec(memory_space=pl.ANY)
    return pl.pallas_call(
        apply_kernel,
        out_shape=(
            jax.ShapeDtypeStruct((28, 512), f32),
            jax.ShapeDtypeStruct((448, 896), f32),
            jax.ShapeDtypeStruct((16, 320), f32),
            jax.ShapeDtypeStruct((320, 448), f32),
        ),
        in_specs=[pl.BlockSpec(memory_space=pltpu.SMEM)] + [anywhere] * 6,
        out_specs=(anywhere,) * 4,
        scratch_shapes=[
            pltpu.VMEM((512, 512), f32),
            pltpu.VMEM((16, 28, 512), f32),
            pltpu.VMEM((32, 48, 512), f32),
            pltpu.VMEM((28, 512), f32),
            pltpu.VMEM((448, 896), f32),
            pltpu.VMEM((320, 448), f32),
            pltpu.VMEM((512, 512), bf16),
            pltpu.VMEM((512, 512), bf16),
            pltpu.VMEM((448, 512), f32),
            pltpu.VMEM((1248, 512), f32),
            pltpu.VMEM((1248, 512), bf16),
            pltpu.VMEM((1248, 512), bf16),
            pltpu.VMEM((28, 512), f32),
            pltpu.VMEM((16, 320), f32),
            pltpu.SemaphoreType.DMA((6,)),
            pltpu.SemaphoreType.DMA((7,)),
        ],
        compiler_params=pltpu.CompilerParams(vmem_limit_bytes=48 * 2**20),
        cost_estimate=pl.CostEstimate(flops=4 * 10**9, bytes_accessed=10**7, transcendentals=0),
        name="apply_inverse",
    )(column, inverse, dealt, gathered, panel, trailing, rest)


def per_device(diag_block, panel, trailing, truth_panel, truth_rest):
    rows, columns = ("x", "y"), ("z", "k")
    packed = jnp.concatenate(
        [
            jnp.pad(panel, ((0, 4), (0, 0))),
            jnp.pad(truth_panel.T, ((0, 0), (0, 192))),
        ],
        0,
    )
    gathered = lax.all_gather(packed, columns, axis=0, tiled=False)
    pieces = spread(diag_block.reshape(4, 128), columns, 32)
    strip = pieces.reshape(32, 4, 8, 16).transpose(1, 2, 0, 3).reshape(32, 512)
    whole = spread(strip, rows, 16).reshape(512, 512)
    copies = jnp.broadcast_to(panel[None], (16, 28, 512))
    copies, whole = lax.optimization_barrier((copies, whole))
    dealt = lax.all_to_all(copies, rows, 0, 0)
    inverse = invert_factor(whole)
    column = (lax.axis_index("z") * 2 + lax.axis_index("k")).astype(jnp.int32)[None]
    factor, updated, solved, truth_updated = apply_inverse(
        column, inverse, dealt, gathered, panel, trailing.T, truth_rest
    )
    return factor, updated.T, solved.T, truth_updated


def solution(mesh):
    fine = jax.sharding.Mesh(mesh.devices.reshape(4, 4, 16, 2), ("x", "y", "z", "k"))
    rows, columns = ("x", "y"), ("z", "k")
    tiled, whole = P(rows, columns), P(rows + columns, None)
    return jax.shard_map(
        per_device,
        mesh=fine,
        in_specs=(tiled, whole, tiled, tiled, tiled),
        out_specs=(whole, tiled, tiled, tiled),
        check_vma=False,
    )
```

```python
import jax
import jax.numpy as jnp
from jax import lax
from jax.experimental import pallas as pl
from jax.experimental.pallas import tpu as pltpu
from jax.sharding import PartitionSpec as P

HI = lax.Precision.HIGHEST
NT = (((1,), (1,)), ((), ()))
NN = (((1,), (0,)), ((), ()))


def halves(value):
    high = value.astype(jnp.bfloat16)
    return high, (value - high.astype(jnp.float32)).astype(jnp.bfloat16)


def factor_tile(d_ref, o_ref):
    n = 16
    lane = lax.broadcasted_iota(jnp.int32, (8, 128), 1)
    sub = lax.broadcasted_iota(jnp.int32, (8, 128), 0)
    full = lambda v: jnp.broadcast_to(v, (8, 128))
    m = [d_ref[8 * i:8 * i + 8, :] for i in range(n)]
    own = [full(m[0][:, c:c + 1]) for c in range(8)]
    for j in range(n):
        lo = 8 * j
        here = (lane >= lo) & (lane < lo + 8)
        s = {(a, c): full(own[c][a:a + 1, :]) for c in range(8) for a in range(c, 8)}
        rows = jnp.where(here, jnp.where(lane - lo == sub, 1.0, 0.0), m[j])
        r = [full(rows[a:a + 1, :]) for a in range(8)]
        if j + 1 < n:
            raw = [full(m[j + 1][:, lo + c:lo + c + 1]) for c in range(8)]
            own = [full(m[j + 1][:, lo + 8 + c:lo + 9 + c]) for c in range(8)]
            t = list(raw)
            near = jnp.where(here, 0.0, m[j + 1])
        l, inv, u = {}, [], []
        for c in range(8):
            q = lax.rsqrt(s[c, c])
            inv.append(q)
            for a in range(c + 1, 8):
                l[a, c] = s[a, c] * q
            for a in range(c + 1, 8):
                for b in range(c + 1, a + 1):
                    s[a, b] = s[a, b] - l[a, c] * l[b, c]
            u.append(r[c] * q)
            for a in range(c + 1, 8):
                r[a] = r[a] - l[a, c] * u[c]
            if j + 1 < n:
                t[c] = t[c] * q
                for a in range(c + 1, 8):
                    t[a] = t[a] - t[c] * l[a, c]
                for a in range(8):
                    own[a] = own[a] - t[c] * full(t[c][a:a + 1, :])
                near = near - t[c] * u[c]
        done = u[0]
        for a in range(1, 8):
            done = jnp.where(sub == a, u[a], done)
        o_ref[lo:lo + 8, :] = jnp.where(lane < lo + 8, done, 0.0)
        if j + 1 < n:
            m[j + 1] = near
        if j + 2 < n:
            v = [None] * 8
            for c in range(7, -1, -1):
                x = u[c]
                for a in range(7, c, -1):
                    x = x - l[a, c] * v[a]
                v[c] = x * inv[c]
            for i in range(j + 2, n):
                acc = jnp.where(here, 0.0, m[i])
                for c in range(8):
                    acc = acc - full(m[i][:, lo + c:lo + c + 1]) * v[c]
                m[i] = acc


def invert_kernel(a_hbm, high_hbm, low_hbm, m_ref, d_ref, t_ref, o_ref, high_ref, low_ref, sem):
    nb, n = 128, 512
    load = pltpu.make_async_copy(a_hbm, m_ref, sem.at[0])
    load.start()
    load.wait()
    dot = lambda p, q, dims: lax.dot_general(p, q, dims, precision=HI, preferred_element_type=jnp.float32)

    def after(k):
        lo, hi = k * nb, (k + 1) * nb
        t = t_ref[...]
        o_ref[lo:hi, lo:hi] = t
        if lo:
            o_ref[lo:hi, :lo] = dot(t, m_ref[lo:hi, :lo], NN)
        if hi < n:
            o_ref[lo:hi, hi:] = jnp.zeros((nb, n - hi), jnp.float32)
            left = dot(m_ref[hi:, lo:hi], t, NT)
            m_ref[hi:, hi:] = m_ref[hi:, hi:] - dot(left, left, NT)
            m_ref[hi:, lo:hi] = -dot(left, t, NN)
            if lo:
                m_ref[hi:, :lo] = m_ref[hi:, :lo] - dot(left, o_ref[lo:hi, :lo], NN)

    def step(k, carry):
        at = pl.ds(pl.multiple_of(k * nb, nb), nb)
        d_ref[...] = m_ref[at, at]
        factor_tile(d_ref, t_ref)
        for i in range(n // nb):
            pl.when(k == i)(lambda i=i: after(i))
        return carry

    lax.fori_loop(0, n // nb, step, 0)
    high_ref[...], low_ref[...] = halves(o_ref[...])
    stores = [
        pltpu.make_async_copy(high_ref, high_hbm, sem.at[1]),
        pltpu.make_async_copy(low_ref, low_hbm, sem.at[2]),
    ]
    for store in stores:
        store.start()
    for store in stores:
        store.wait()


def invert_factor(block):
    n = block.shape[0]
    anywhere = pl.BlockSpec(memory_space=pl.ANY)
    half = jax.ShapeDtypeStruct((n, n), jnp.bfloat16)
    return pl.pallas_call(
        invert_kernel,
        out_shape=(half, half),
        in_specs=[anywhere],
        out_specs=(anywhere, anywhere),
        scratch_shapes=[
            pltpu.VMEM((n, n), jnp.float32),
            pltpu.VMEM((128, 128), jnp.float32),
            pltpu.VMEM((128, 128), jnp.float32),
            pltpu.VMEM((n, n), jnp.float32),
            pltpu.VMEM((n, n), jnp.bfloat16),
            pltpu.VMEM((n, n), jnp.bfloat16),
            pltpu.SemaphoreType.DMA((3,)),
        ],
        compiler_params=pltpu.CompilerParams(vmem_limit_bytes=16 * 2**20),
        cost_estimate=pl.CostEstimate(flops=10**10, bytes_accessed=2 * 10**6, transcendentals=0),
        name="invert_factor",
    )(block)


def spread(value, axes, count):
    copies = jnp.broadcast_to(value[None], (count,) + value.shape)
    return lax.all_to_all(copies, axes, 0, 0)


def thrice(a_high, a_low, b_high, b_low, dims):
    dot = lambda p, q: lax.dot_general(p, q, dims, preferred_element_type=jnp.float32)
    return dot(a_high, b_high) + dot(a_high, b_low) + dot(a_low, b_high)


def apply_kernel(
    col_ref, high_hbm, low_hbm, dealt_hbm, gathered_hbm, panel_hbm, trailing_hbm, rest_hbm,
    factor_hbm, updated_hbm, solved_hbm, truth_hbm,
    inv_high, inv_low, dealt, gathered, panel, trailing, rest,
    row_high, row_low, x_high, x_low, factor, solved, sem, out_sem,
):
    loads = [
        pltpu.make_async_copy(src, dst, sem.at[i])
        for i, (src, dst) in enumerate(
            [
                (high_hbm, inv_high), (low_hbm, inv_low), (dealt_hbm, dealt), (gathered_hbm, gathered),
                (panel_hbm, panel), (trailing_hbm, trailing), (rest_hbm, rest),
            ]
        )
    ]
    for load in loads:
        load.start()
    loads[0].wait()
    loads[1].wait()

    def solve(high, low):
        a = thrice(high[:, :256], low[:, :256], inv_high[:256, :256], inv_low[:256, :256], NT)
        b = thrice(high, low, inv_high[256:, :], inv_low[256:, :], NT)
        return jnp.concatenate([a, b], 1)

    loads[2].wait()
    for r in range(16):
        row_high[28 * r:28 * r + 28, :] = dealt[r]
    high, low = halves(row_high[...])
    done = solve(high, low)
    d_high, d_low = halves(done)
    loads[3].wait()
    loads[4].wait()
    stack = row_low
    for c in range(32):
        stack[28 * c:28 * c + 28, :] = gathered[c, 0:28, :]
    truth = gathered[:, 32:48, 0:384].reshape(512, 384)
    stack[896:1216, :] = truth.T[0:320, :]
    stack[1216:1244, :] = panel[...]
    stack[1244:1248, :] = jnp.zeros((4, 512), jnp.float32)
    at = pl.ds(pl.multiple_of(col_ref[0] * 16, 16), 16)
    i_high, i_low = inv_high[at, :], inv_low[at, :]
    t_high, t_low = halves(stack[896:1216, :])
    solved[...] = thrice(i_high, i_low, t_high, t_low, NT)
    for lo, hi in ((0, 416), (416, 832), (832, 1248)):
        high, low = halves(stack[lo:hi, :])
        part = solve(high, low)
        if hi == 1248:
            factor[...] = part[1216 - lo:1244 - lo, :]
        x_high[lo:hi, :], x_low[lo:hi, :] = halves(part)
    stores = [
        pltpu.make_async_copy(factor, factor_hbm, out_sem.at[0]),
        pltpu.make_async_copy(solved, solved_hbm, out_sem.at[1]),
    ]
    for store in stores:
        store.start()
    loads[5].wait()
    for i in range(4):
        a = slice(112 * i, 112 * i + 112)
        trailing[a, :] = trailing[a, :] - thrice(d_high[a], d_low[a], x_high[:896, :], x_low[:896, :], NT)
        store = pltpu.make_async_copy(trailing.at[a], updated_hbm.at[a], out_sem.at[2 + i])
        store.start()
        stores.append(store)
    loads[6].wait()
    rest[...] = rest[...] - thrice(x_high[896:1216, :], x_low[896:1216, :], d_high, d_low, NT)
    store = pltpu.make_async_copy(rest, truth_hbm, out_sem.at[6])
    store.start()
    stores.append(store)
    for store in stores:
        store.wait()


def apply_inverse(column, high, low, dealt, gathered, panel, trailing, rest):
    f32, bf16 = jnp.float32, jnp.bfloat16
    anywhere = pl.BlockSpec(memory_space=pl.ANY)
    keep = pltpu.with_memory_space_constraint
    return pl.pallas_call(
        apply_kernel,
        out_shape=(
            jax.ShapeDtypeStruct((28, 512), f32),
            jax.ShapeDtypeStruct((448, 896), f32),
            jax.ShapeDtypeStruct((16, 320), f32),
            jax.ShapeDtypeStruct((320, 448), f32),
        ),
        in_specs=[pl.BlockSpec(memory_space=pltpu.SMEM)] + [anywhere] * 3 + [pl.BlockSpec(memory_space=pltpu.HBM)] * 4,
        out_specs=(pl.BlockSpec(memory_space=pltpu.HBM),) * 4,
        scratch_shapes=[
            pltpu.VMEM((512, 512), bf16),
            pltpu.VMEM((512, 512), bf16),
            pltpu.VMEM((16, 28, 512), f32),
            pltpu.VMEM((32, 48, 512), f32),
            pltpu.VMEM((28, 512), f32),
            pltpu.VMEM((448, 896), f32),
            pltpu.VMEM((320, 448), f32),
            pltpu.VMEM((448, 512), f32),
            pltpu.VMEM((1248, 512), f32),
            pltpu.VMEM((1248, 512), bf16),
            pltpu.VMEM((1248, 512), bf16),
            pltpu.VMEM((28, 512), f32),
            pltpu.VMEM((16, 320), f32),
            pltpu.SemaphoreType.DMA((7,)),
            pltpu.SemaphoreType.DMA((7,)),
        ],
        compiler_params=pltpu.CompilerParams(vmem_limit_bytes=24 * 2**20),
        cost_estimate=pl.CostEstimate(flops=4 * 10**9, bytes_accessed=10**7, transcendentals=0),
        name="apply_inverse",
    )(column, high, low, dealt, *(keep(x, pltpu.HBM) for x in (gathered, panel, trailing, rest)))


def per_device(diag_block, panel, trailing, truth_panel, truth_rest):
    rows, columns = ("x", "y"), ("z", "k")
    packed = jnp.concatenate(
        [
            jnp.pad(panel, ((0, 4), (0, 0))),
            jnp.pad(truth_panel.T, ((0, 0), (0, 192))),
        ],
        0,
    )
    gathered = lax.all_gather(packed, columns, axis=0, tiled=False)
    pieces = spread(diag_block.reshape(4, 128), columns, 32)
    strip = pieces.reshape(32, 4, 8, 16).transpose(1, 2, 0, 3).reshape(32, 512)
    whole = spread(strip, rows, 16).reshape(512, 512)
    copies = jnp.broadcast_to(panel[None], (16, 28, 512))
    copies, whole = lax.optimization_barrier((copies, whole))
    dealt = lax.all_to_all(copies, rows, 0, 0)
    high, low = invert_factor(whole)
    column = (lax.axis_index("z") * 2 + lax.axis_index("k")).astype(jnp.int32)[None]
    factor, updated, solved, truth_updated = apply_inverse(
        column, high, low, dealt, gathered, panel, trailing.T, truth_rest
    )
    return factor, updated.T, solved.T, truth_updated


def solution(mesh):
    fine = jax.sharding.Mesh(mesh.devices.reshape(4, 4, 16, 2), ("x", "y", "z", "k"))
    rows, columns = ("x", "y"), ("z", "k")
    tiled, whole = P(rows, columns), P(rows + columns, None)
    return jax.shard_map(
        per_device,
        mesh=fine,
        in_specs=(tiled, whole, tiled, tiled, tiled),
        out_specs=(whole, tiled, tiled, tiled),
        check_vma=False,
    )
```

```python
import jax
import jax.numpy as jnp
from jax import lax
from jax.experimental import pallas as pl
from jax.experimental.pallas import tpu as pltpu
from jax.sharding import PartitionSpec as P

HI = lax.Precision.HIGHEST
NT = (((1,), (1,)), ((), ()))
NN = (((1,), (0,)), ((), ()))


def halves(value):
    high = value.astype(jnp.bfloat16)
    return high, (value - high.astype(jnp.float32)).astype(jnp.bfloat16)


def factor_tile(d_ref, o_ref):
    n = 16
    lane = lax.broadcasted_iota(jnp.int32, (8, 128), 1)
    sub = lax.broadcasted_iota(jnp.int32, (8, 128), 0)
    full = lambda v: jnp.broadcast_to(v, (8, 128))
    m = [d_ref[8 * i:8 * i + 8, :] for i in range(n)]
    own = [full(m[0][:, c:c + 1]) for c in range(8)]
    for j in range(n):
        lo = 8 * j
        here = (lane >= lo) & (lane < lo + 8)
        s = {(a, c): full(own[c][a:a + 1, :]) for c in range(8) for a in range(c, 8)}
        rows = jnp.where(here, jnp.where(lane - lo == sub, 1.0, 0.0), m[j])
        r = [full(rows[a:a + 1, :]) for a in range(8)]
        if j + 1 < n:
            raw = [full(m[j + 1][:, lo + c:lo + c + 1]) for c in range(8)]
            own = [full(m[j + 1][:, lo + 8 + c:lo + 9 + c]) for c in range(8)]
            t = list(raw)
            near = jnp.where(here, 0.0, m[j + 1])
        l, inv, u = {}, [], []
        for c in range(8):
            q = lax.rsqrt(s[c, c])
            inv.append(q)
            for a in range(c + 1, 8):
                l[a, c] = s[a, c] * q
            for a in range(c + 1, 8):
                for b in range(c + 1, a + 1):
                    s[a, b] = s[a, b] - l[a, c] * l[b, c]
            u.append(r[c] * q)
            for a in range(c + 1, 8):
                r[a] = r[a] - l[a, c] * u[c]
            if j + 1 < n:
                t[c] = t[c] * q
                for a in range(c + 1, 8):
                    t[a] = t[a] - t[c] * l[a, c]
                for a in range(8):
                    own[a] = own[a] - t[c] * full(t[c][a:a + 1, :])
                near = near - t[c] * u[c]
        done = u[0]
        for a in range(1, 8):
            done = jnp.where(sub == a, u[a], done)
        o_ref[lo:lo + 8, :] = jnp.where(lane < lo + 8, done, 0.0)
        if j + 1 < n:
            m[j + 1] = near
        if j + 2 < n:
            v = [None] * 8
            for c in range(7, -1, -1):
                x = u[c]
                for a in range(7, c, -1):
                    x = x - l[a, c] * v[a]
                v[c] = x * inv[c]
            for i in range(j + 2, n):
                acc = jnp.where(here, 0.0, m[i])
                for c in range(8):
                    acc = acc - full(m[i][:, lo + c:lo + c + 1]) * v[c]
                m[i] = acc


def invert_kernel(a_hbm, high_hbm, low_hbm, m_ref, d_ref, t_ref, o_ref, high_ref, low_ref, sem):
    nb, n = 128, 512
    load = pltpu.make_async_copy(a_hbm, m_ref, sem.at[0])
    load.start()
    load.wait()
    dot = lambda p, q, dims: lax.dot_general(p, q, dims, precision=HI, preferred_element_type=jnp.float32)

    def after(k):
        lo, hi = k * nb, (k + 1) * nb
        t = t_ref[...]
        o_ref[lo:hi, lo:hi] = t
        if lo:
            o_ref[lo:hi, :lo] = dot(t, m_ref[lo:hi, :lo], NN)
        if hi < n:
            o_ref[lo:hi, hi:] = jnp.zeros((nb, n - hi), jnp.float32)
            left = dot(m_ref[hi:, lo:hi], t, NT)
            m_ref[hi:, hi:] = m_ref[hi:, hi:] - dot(left, left, NT)
            m_ref[hi:, lo:hi] = -dot(left, t, NN)
            if lo:
                m_ref[hi:, :lo] = m_ref[hi:, :lo] - dot(left, o_ref[lo:hi, :lo], NN)

    def step(k, carry):
        at = pl.ds(pl.multiple_of(k * nb, nb), nb)
        d_ref[...] = m_ref[at, at]
        factor_tile(d_ref, t_ref)
        for i in range(n // nb):
            pl.when(k == i)(lambda i=i: after(i))
        return carry

    lax.fori_loop(0, n // nb, step, 0)
    high_ref[...], low_ref[...] = halves(o_ref[...])
    stores = [
        pltpu.make_async_copy(high_ref, high_hbm, sem.at[1]),
        pltpu.make_async_copy(low_ref, low_hbm, sem.at[2]),
    ]
    for store in stores:
        store.start()
    for store in stores:
        store.wait()


def invert_factor(block):
    n = block.shape[0]
    anywhere = pl.BlockSpec(memory_space=pl.ANY)
    half = jax.ShapeDtypeStruct((n, n), jnp.bfloat16)
    return pl.pallas_call(
        invert_kernel,
        out_shape=(half, half),
        in_specs=[anywhere],
        out_specs=(anywhere, anywhere),
        scratch_shapes=[
            pltpu.VMEM((n, n), jnp.float32),
            pltpu.VMEM((128, 128), jnp.float32),
            pltpu.VMEM((128, 128), jnp.float32),
            pltpu.VMEM((n, n), jnp.float32),
            pltpu.VMEM((n, n), jnp.bfloat16),
            pltpu.VMEM((n, n), jnp.bfloat16),
            pltpu.SemaphoreType.DMA((3,)),
        ],
        compiler_params=pltpu.CompilerParams(vmem_limit_bytes=16 * 2**20),
        cost_estimate=pl.CostEstimate(flops=10**10, bytes_accessed=2 * 10**6, transcendentals=0),
        name="invert_factor",
    )(block)


def pack_kernel(panel_ref, truth_ref, packed_ref, copies_hbm, sem):
    copies = [pltpu.make_async_copy(panel_ref, copies_hbm.at[i], sem.at[i]) for i in range(16)]
    for copy in copies:
        copy.start()
    packed_ref[0:8, 0:256] = truth_ref[0:8, 0:256]
    packed_ref[0:8, 256:512] = truth_ref[8:16, 0:256]
    packed_ref[8:12, :] = jnp.zeros((4, 512), jnp.float32)
    for q in range(4):
        packed_ref[8:12, 128 * q:128 * q + 64] = truth_ref[4 * q:4 * q + 4, 256:320]
    packed_ref[12:40, :] = panel_ref[...]
    for copy in copies:
        copy.wait()


def pack(panel, truth):
    f32 = jnp.float32
    whole = pl.BlockSpec(memory_space=pltpu.VMEM)
    return pl.pallas_call(
        pack_kernel,
        out_shape=(jax.ShapeDtypeStruct((40, 512), f32), jax.ShapeDtypeStruct((16, 28, 512), f32)),
        in_specs=[whole, whole],
        out_specs=(whole, pl.BlockSpec(memory_space=pl.ANY)),
        scratch_shapes=[pltpu.SemaphoreType.DMA((16,))],
        compiler_params=pltpu.CompilerParams(vmem_limit_bytes=4 * 2**20),
        name="pack",
    )(panel, truth)


def copy_kernel(strip_ref, copies_hbm, sem):
    copies = [pltpu.make_async_copy(strip_ref, copies_hbm.at[i], sem.at[i]) for i in range(16)]
    for copy in copies:
        copy.start()
    for copy in copies:
        copy.wait()


def copy_out(strip):
    return pl.pallas_call(
        copy_kernel,
        out_shape=jax.ShapeDtypeStruct((16,) + strip.shape, strip.dtype),
        in_specs=[pl.BlockSpec(memory_space=pltpu.VMEM)],
        out_specs=pl.BlockSpec(memory_space=pl.ANY),
        scratch_shapes=[pltpu.SemaphoreType.DMA((16,))],
        compiler_params=pltpu.CompilerParams(vmem_limit_bytes=4 * 2**20),
        name="copy_out",
    )(strip)


def thrice(a_high, a_low, b_high, b_low, dims):
    dot = lambda p, q: lax.dot_general(p, q, dims, preferred_element_type=jnp.float32)
    return dot(a_high, b_high) + dot(a_high, b_low) + dot(a_low, b_high)


def apply_kernel(
    col_ref, high_hbm, low_hbm, dealt_hbm, gathered_hbm, panel_hbm, trailing_hbm, rest_hbm,
    factor_hbm, updated_hbm, solved_hbm, truth_hbm,
    inv_high, inv_low, dealt, gathered, panel, trailing, rest,
    row_high, row_low, truth, x_high, x_low, factor, solved, sem, out_sem,
):
    loads = [
        pltpu.make_async_copy(src, dst, sem.at[i])
        for i, (src, dst) in enumerate(
            [
                (high_hbm, inv_high), (low_hbm, inv_low), (dealt_hbm, dealt), (gathered_hbm, gathered),
                (panel_hbm, panel), (trailing_hbm, trailing), (rest_hbm, rest),
            ]
        )
    ]
    for load in loads:
        load.start()
    loads[0].wait()
    loads[1].wait()

    def solve(high, low):
        a = thrice(high[:, :256], low[:, :256], inv_high[:256, :256], inv_low[:256, :256], NT)
        b = thrice(high, low, inv_high[256:, :], inv_low[256:, :], NT)
        return jnp.concatenate([a, b], 1)

    loads[2].wait()
    for r in range(16):
        row_high[28 * r:28 * r + 28, :] = dealt[r]
    high, low = halves(row_high[...])
    done = solve(high, low)
    d_high, d_low = halves(done)
    loads[3].wait()
    loads[4].wait()
    stack = row_low
    for c in range(32):
        stack[28 * c:28 * c + 28, :] = gathered[c, 12:40, :]
        truth[16 * c:16 * c + 8, 0:256] = gathered[c, 0:8, 0:256]
        truth[16 * c + 8:16 * c + 16, 0:256] = gathered[c, 0:8, 256:512]
        for q in range(4):
            truth[16 * c + 4 * q:16 * c + 4 * q + 4, 256:384] = gathered[c, 8:12, 128 * q:128 * q + 128]
    stack[896:1216, :] = truth[...].T[0:320, :]
    stack[1216:1244, :] = panel[...]
    stack[1244:1248, :] = jnp.zeros((4, 512), jnp.float32)
    at = pl.ds(pl.multiple_of(col_ref[0] * 16, 16), 16)
    i_high, i_low = inv_high[at, :], inv_low[at, :]
    t_high, t_low = halves(stack[896:1216, :])
    solved[...] = thrice(i_high, i_low, t_high, t_low, NT)
    for lo, hi in ((0, 416), (416, 832), (832, 1248)):
        high, low = halves(stack[lo:hi, :])
        part = solve(high, low)
        if hi == 1248:
            factor[...] = part[1216 - lo:1244 - lo, :]
        x_high[lo:hi, :], x_low[lo:hi, :] = halves(part)
    stores = [
        pltpu.make_async_copy(factor, factor_hbm, out_sem.at[0]),
        pltpu.make_async_copy(solved, solved_hbm, out_sem.at[1]),
    ]
    for store in stores:
        store.start()
    loads[5].wait()
    for i in range(4):
        a = slice(112 * i, 112 * i + 112)
        trailing[a, :] = trailing[a, :] - thrice(d_high[a], d_low[a], x_high[:896, :], x_low[:896, :], NT)
        store = pltpu.make_async_copy(trailing.at[a], updated_hbm.at[a], out_sem.at[2 + i])
        store.start()
        stores.append(store)
    loads[6].wait()
    rest[...] = rest[...] - thrice(x_high[896:1216, :], x_low[896:1216, :], d_high, d_low, NT)
    store = pltpu.make_async_copy(rest, truth_hbm, out_sem.at[6])
    store.start()
    stores.append(store)
    for store in stores:
        store.wait()


def apply_inverse(column, high, low, dealt, gathered, panel, trailing, rest):
    f32, bf16 = jnp.float32, jnp.bfloat16
    anywhere = pl.BlockSpec(memory_space=pl.ANY)
    keep = pltpu.with_memory_space_constraint
    return pl.pallas_call(
        apply_kernel,
        out_shape=(
            jax.ShapeDtypeStruct((28, 512), f32),
            jax.ShapeDtypeStruct((448, 896), f32),
            jax.ShapeDtypeStruct((16, 320), f32),
            jax.ShapeDtypeStruct((320, 448), f32),
        ),
        in_specs=[pl.BlockSpec(memory_space=pltpu.SMEM)] + [anywhere] * 3 + [pl.BlockSpec(memory_space=pltpu.HBM)] * 4,
        out_specs=(pl.BlockSpec(memory_space=pltpu.HBM),) * 4,
        scratch_shapes=[
            pltpu.VMEM((512, 512), bf16),
            pltpu.VMEM((512, 512), bf16),
            pltpu.VMEM((16, 28, 512), f32),
            pltpu.VMEM((32, 40, 512), f32),
            pltpu.VMEM((28, 512), f32),
            pltpu.VMEM((448, 896), f32),
            pltpu.VMEM((320, 448), f32),
            pltpu.VMEM((448, 512), f32),
            pltpu.VMEM((1248, 512), f32),
            pltpu.VMEM((512, 384), f32),
            pltpu.VMEM((1248, 512), bf16),
            pltpu.VMEM((1248, 512), bf16),
            pltpu.VMEM((28, 512), f32),
            pltpu.VMEM((16, 320), f32),
            pltpu.SemaphoreType.DMA((7,)),
            pltpu.SemaphoreType.DMA((7,)),
        ],
        compiler_params=pltpu.CompilerParams(vmem_limit_bytes=24 * 2**20),
        cost_estimate=pl.CostEstimate(flops=4 * 10**9, bytes_accessed=10**7, transcendentals=0),
        name="apply_inverse",
    )(column, high, low, dealt, *(keep(x, pltpu.HBM) for x in (gathered, panel, trailing, rest)))


def per_device(diag_block, panel, trailing, truth_panel, truth_rest):
    rows, columns = ("x", "y"), ("z", "k")
    packed, copies = pack(panel, truth_panel.T)
    gathered = lax.all_gather(packed, columns, axis=0, tiled=False)
    small = jnp.broadcast_to(diag_block.reshape(1, 4, 128), (32, 4, 128))
    pieces = lax.all_to_all(small, columns, 0, 0)
    strip = pieces.reshape(32, 4, 8, 16).transpose(1, 2, 0, 3).reshape(32, 512)
    whole = lax.all_to_all(copy_out(strip), rows, 0, 0).reshape(512, 512)
    copies, whole = lax.optimization_barrier((copies, whole))
    dealt = lax.all_to_all(copies, rows, 0, 0)
    high, low = invert_factor(whole)
    column = (lax.axis_index("z") * 2 + lax.axis_index("k")).astype(jnp.int32)[None]
    factor, updated, solved, truth_updated = apply_inverse(
        column, high, low, dealt, gathered, panel, trailing.T, truth_rest
    )
    return factor, updated.T, solved.T, truth_updated


def solution(mesh):
    fine = jax.sharding.Mesh(mesh.devices.reshape(4, 4, 16, 2), ("x", "y", "z", "k"))
    rows, columns = ("x", "y"), ("z", "k")
    tiled, whole = P(rows, columns), P(rows + columns, None)
    return jax.shard_map(
        per_device,
        mesh=fine,
        in_specs=(tiled, whole, tiled, tiled, tiled),
        out_specs=(whole, tiled, tiled, tiled),
        check_vma=False,
    )
```

```python
import jax
import jax.numpy as jnp
from jax import lax
from jax.experimental import pallas as pl
from jax.experimental.pallas import tpu as pltpu
from jax.sharding import PartitionSpec as P

HI = lax.Precision.HIGHEST
NT = (((1,), (1,)), ((), ()))
NN = (((1,), (0,)), ((), ()))


def halves(value):
    high = value.astype(jnp.bfloat16)
    return high, (value - high.astype(jnp.float32)).astype(jnp.bfloat16)


def factor_tile(d_ref, o_ref):
    n = 16
    lane = lax.broadcasted_iota(jnp.int32, (8, 128), 1)
    sub = lax.broadcasted_iota(jnp.int32, (8, 128), 0)
    full = lambda v: jnp.broadcast_to(v, (8, 128))
    m = [d_ref[8 * i:8 * i + 8, :] for i in range(n)]
    own = [full(m[0][:, c:c + 1]) for c in range(8)]
    for j in range(n):
        lo = 8 * j
        here = (lane >= lo) & (lane < lo + 8)
        s = {(a, c): full(own[c][a:a + 1, :]) for c in range(8) for a in range(c, 8)}
        rows = jnp.where(here, jnp.where(lane - lo == sub, 1.0, 0.0), m[j])
        r = [full(rows[a:a + 1, :]) for a in range(8)]
        if j + 1 < n:
            raw = [full(m[j + 1][:, lo + c:lo + c + 1]) for c in range(8)]
            own = [full(m[j + 1][:, lo + 8 + c:lo + 9 + c]) for c in range(8)]
            t = list(raw)
            near = jnp.where(here, 0.0, m[j + 1])
        l, inv, u = {}, [], []
        for c in range(8):
            q = lax.rsqrt(s[c, c])
            inv.append(q)
            for a in range(c + 1, 8):
                l[a, c] = s[a, c] * q
            for a in range(c + 1, 8):
                for b in range(c + 1, a + 1):
                    s[a, b] = s[a, b] - l[a, c] * l[b, c]
            u.append(r[c] * q)
            for a in range(c + 1, 8):
                r[a] = r[a] - l[a, c] * u[c]
            if j + 1 < n:
                t[c] = t[c] * q
                for a in range(c + 1, 8):
                    t[a] = t[a] - t[c] * l[a, c]
                for a in range(8):
                    own[a] = own[a] - t[c] * full(t[c][a:a + 1, :])
                near = near - t[c] * u[c]
        done = u[0]
        for a in range(1, 8):
            done = jnp.where(sub == a, u[a], done)
        o_ref[lo:lo + 8, :] = jnp.where(lane < lo + 8, done, 0.0)
        if j + 1 < n:
            m[j + 1] = near
        if j + 2 < n:
            v = [None] * 8
            for c in range(7, -1, -1):
                x = u[c]
                for a in range(7, c, -1):
                    x = x - l[a, c] * v[a]
                v[c] = x * inv[c]
            for i in range(j + 2, n):
                acc = jnp.where(here, 0.0, m[i])
                for c in range(8):
                    acc = acc - full(m[i][:, lo + c:lo + c + 1]) * v[c]
                m[i] = acc


def invert_kernel(a_hbm, high_hbm, low_hbm, m_ref, d_ref, t_ref, o_ref, high_ref, low_ref, sem):
    nb, n = 128, 512
    load = pltpu.make_async_copy(a_hbm, m_ref, sem.at[0])
    load.start()
    load.wait()
    dot = lambda p, q, dims: lax.dot_general(p, q, dims, precision=HI, preferred_element_type=jnp.float32)

    def after(k):
        lo, hi = k * nb, (k + 1) * nb
        t = t_ref[...]
        o_ref[lo:hi, lo:hi] = t
        if lo:
            o_ref[lo:hi, :lo] = dot(t, m_ref[lo:hi, :lo], NN)
        if hi < n:
            o_ref[lo:hi, hi:] = jnp.zeros((nb, n - hi), jnp.float32)
            left = dot(m_ref[hi:, lo:hi], t, NT)
            m_ref[hi:, hi:] = m_ref[hi:, hi:] - dot(left, left, NT)
            m_ref[hi:, lo:hi] = -dot(left, t, NN)
            if lo:
                m_ref[hi:, :lo] = m_ref[hi:, :lo] - dot(left, o_ref[lo:hi, :lo], NN)

    def step(k, carry):
        at = pl.ds(pl.multiple_of(k * nb, nb), nb)
        d_ref[...] = m_ref[at, at]
        factor_tile(d_ref, t_ref)
        for i in range(n // nb):
            pl.when(k == i)(lambda i=i: after(i))
        return carry

    lax.fori_loop(0, n // nb, step, 0)
    high_ref[...], low_ref[...] = halves(o_ref[...])
    stores = [
        pltpu.make_async_copy(high_ref, high_hbm, sem.at[1]),
        pltpu.make_async_copy(low_ref, low_hbm, sem.at[2]),
    ]
    for store in stores:
        store.start()
    for store in stores:
        store.wait()


def invert_factor(block):
    n = block.shape[0]
    anywhere = pl.BlockSpec(memory_space=pl.ANY)
    half = jax.ShapeDtypeStruct((n, n), jnp.bfloat16)
    return pl.pallas_call(
        invert_kernel,
        out_shape=(half, half),
        in_specs=[anywhere],
        out_specs=(anywhere, anywhere),
        scratch_shapes=[
            pltpu.VMEM((n, n), jnp.float32),
            pltpu.VMEM((128, 128), jnp.float32),
            pltpu.VMEM((128, 128), jnp.float32),
            pltpu.VMEM((n, n), jnp.float32),
            pltpu.VMEM((n, n), jnp.bfloat16),
            pltpu.VMEM((n, n), jnp.bfloat16),
            pltpu.SemaphoreType.DMA((3,)),
        ],
        compiler_params=pltpu.CompilerParams(vmem_limit_bytes=16 * 2**20),
        cost_estimate=pl.CostEstimate(flops=10**10, bytes_accessed=2 * 10**6, transcendentals=0),
        name="invert_factor",
    )(block)


def pack_kernel(panel_hbm, truth_hbm, packed_hbm, panel, truth, packed, sem):
    first = pltpu.make_async_copy(panel_hbm, panel, sem.at[0])
    second = pltpu.make_async_copy(truth_hbm, truth, sem.at[1])
    first.start()
    second.start()
    second.wait()
    packed[28:32, :] = jnp.zeros((4, 512), jnp.float32)
    for q in range(4):
        packed[28:32, 128 * q:128 * q + 64] = truth[4 * q:4 * q + 4, 256:320]
    packed[32:40, 0:256] = truth[0:8, 0:256]
    packed[32:40, 256:512] = truth[8:16, 0:256]
    first.wait()
    packed[0:28, :] = panel[...]
    store = pltpu.make_async_copy(packed, packed_hbm, sem.at[2])
    store.start()
    store.wait()


def pack(panel, truth):
    f32 = jnp.float32
    hbm = pl.BlockSpec(memory_space=pltpu.HBM)
    keep = pltpu.with_memory_space_constraint
    return pl.pallas_call(
        pack_kernel,
        out_shape=jax.ShapeDtypeStruct((40, 512), f32),
        in_specs=[hbm, hbm],
        out_specs=hbm,
        scratch_shapes=[
            pltpu.VMEM((28, 512), f32),
            pltpu.VMEM((16, 320), f32),
            pltpu.VMEM((40, 512), f32),
            pltpu.SemaphoreType.DMA((3,)),
        ],
        compiler_params=pltpu.CompilerParams(vmem_limit_bytes=2 * 2**20),
        name="pack",
    )(keep(panel, pltpu.HBM), keep(truth, pltpu.HBM))


def copy_kernel(strip_ref, copies_hbm, sem):
    copies = [pltpu.make_async_copy(strip_ref, copies_hbm.at[i], sem.at[i]) for i in range(16)]
    for copy in copies:
        copy.start()
    for copy in copies:
        copy.wait()


def copy_out(strip):
    return pl.pallas_call(
        copy_kernel,
        out_shape=jax.ShapeDtypeStruct((16,) + strip.shape, strip.dtype),
        in_specs=[pl.BlockSpec(memory_space=pltpu.VMEM)],
        out_specs=pl.BlockSpec(memory_space=pl.ANY),
        scratch_shapes=[pltpu.SemaphoreType.DMA((16,))],
        compiler_params=pltpu.CompilerParams(vmem_limit_bytes=4 * 2**20),
        name="copy_out",
    )(strip)


def thrice(a, b, dims):
    dot = lambda p, q: lax.dot_general(p, q, dims, preferred_element_type=jnp.float32)
    return dot(a[0], b[0]) + dot(a[0], b[1]) + dot(a[1], b[0])


def solve(rows, high, low):
    top = (high[:256, :256], low[:256, :256])
    low_left = (high[256:, :], low[256:, :])
    a = thrice((rows[0][:, :256], rows[1][:, :256]), top, NT)
    return jnp.concatenate([a, thrice(rows, low_left, NT)], 1)


def dealt_kernel(high_any, low_any, dealt_any, panel_hbm, d_high_any, d_low_any, factor_hbm, high, low, dealt, stack, d_high, d_low, factor, sem):
    loads = [
        pltpu.make_async_copy(src, dst, sem.at[i])
        for i, (src, dst) in enumerate(
            [(high_any, high), (low_any, low), (dealt_any, dealt), (panel_hbm, factor)]
        )
    ]
    for load in loads:
        load.start()
    for load in loads:
        load.wait()
    for r in range(16):
        stack[28 * r:28 * r + 28, :] = dealt[r]
    stack[448:476, :] = factor[...]
    stack[476:480, :] = jnp.zeros((4, 512), jnp.float32)
    done = solve(halves(stack[...]), high, low)
    factor[...] = done[448:476, :]
    d_high[...], d_low[...] = halves(done[:448, :])
    stores = [
        pltpu.make_async_copy(src, dst, sem.at[4 + i])
        for i, (src, dst) in enumerate([(factor, factor_hbm), (d_high, d_high_any), (d_low, d_low_any)])
    ]
    for store in stores:
        store.start()
    for store in stores:
        store.wait()


def solve_dealt(high, low, dealt, panel):
    f32, bf16 = jnp.float32, jnp.bfloat16
    anywhere, hbm = pl.BlockSpec(memory_space=pl.ANY), pl.BlockSpec(memory_space=pltpu.HBM)
    half = jax.ShapeDtypeStruct((448, 512), bf16)
    return pl.pallas_call(
        dealt_kernel,
        out_shape=(half, half, jax.ShapeDtypeStruct((28, 512), f32)),
        in_specs=[anywhere] * 3 + [hbm],
        out_specs=(anywhere, anywhere, hbm),
        scratch_shapes=[
            pltpu.VMEM((512, 512), bf16),
            pltpu.VMEM((512, 512), bf16),
            pltpu.VMEM((16, 28, 512), f32),
            pltpu.VMEM((480, 512), f32),
            pltpu.VMEM((448, 512), bf16),
            pltpu.VMEM((448, 512), bf16),
            pltpu.VMEM((28, 512), f32),
            pltpu.SemaphoreType.DMA((7,)),
        ],
        compiler_params=pltpu.CompilerParams(vmem_limit_bytes=12 * 2**20),
        cost_estimate=pl.CostEstimate(flops=10**9, bytes_accessed=2 * 10**6, transcendentals=0),
        name="solve_dealt",
    )(high, low, dealt, pltpu.with_memory_space_constraint(panel, pltpu.HBM))


def apply_kernel(
    col_ref, high_any, low_any, d_high_any, d_low_any, gathered_hbm, trailing_hbm, rest_hbm,
    updated_hbm, solved_hbm, truth_hbm,
    high, low, d_high, d_low, gathered, trailing, rest, stack, truth, solved, sem, out_sem,
):
    loads = [
        pltpu.make_async_copy(src, dst, sem.at[i])
        for i, (src, dst) in enumerate(
            [
                (gathered_hbm.at[0:19], gathered.at[0:19]), (high_any, high), (low_any, low),
                (d_high_any, d_high), (d_low_any, d_low),
                (trailing_hbm, trailing), (gathered_hbm.at[19:32], gathered.at[19:32]), (rest_hbm, rest),
            ]
        )
    ]
    for load in loads:
        load.start()
    for load in loads[:3]:
        load.wait()
    stores = []

    def unpack(first, last):
        for c in range(first, last):
            stack[28 * c:28 * c + 28, :] = gathered[c, 0:28, :]
            truth[16 * c:16 * c + 8, 0:256] = gathered[c, 32:40, 0:256]
            truth[16 * c + 8:16 * c + 16, 0:256] = gathered[c, 32:40, 256:512]
            for q in range(4):
                truth[16 * c + 4 * q:16 * c + 4 * q + 4, 256:384] = gathered[c, 28:32, 128 * q:128 * q + 128]

    def put(src, dst):
        store = pltpu.make_async_copy(src, dst, out_sem.at[len(stores)])
        store.start()
        stores.append(store)

    def update(first, last):
        rows = halves(solve(halves(stack[first:last, :]), high, low))
        dealt = (d_high[...], d_low[...])
        trailing[:, first:last] = trailing[:, first:last] - thrice(dealt, rows, NT)
        put(trailing.at[:, first:last], updated_hbm.at[:, first:last])

    unpack(0, 19)
    for load in loads[3:6]:
        load.wait()
    update(0, 512)
    loads[6].wait()
    unpack(19, 32)
    update(512, 896)
    columns = halves(truth[...].T[0:320, :])
    at = pl.ds(pl.multiple_of(col_ref[0] * 16, 16), 16)
    solved[...] = thrice((high[at, :], low[at, :]), columns, NT)
    put(solved, solved_hbm)
    rows = halves(solve(columns, high, low))
    loads[7].wait()
    rest[...] = rest[...] - thrice(rows, (d_high[...], d_low[...]), NT)
    put(rest, truth_hbm)
    for store in stores:
        store.wait()


def apply_inverse(column, high, low, d_high, d_low, gathered, trailing, rest):
    f32, bf16 = jnp.float32, jnp.bfloat16
    anywhere, hbm = pl.BlockSpec(memory_space=pl.ANY), pl.BlockSpec(memory_space=pltpu.HBM)
    keep = pltpu.with_memory_space_constraint
    return pl.pallas_call(
        apply_kernel,
        out_shape=(
            jax.ShapeDtypeStruct((448, 896), f32),
            jax.ShapeDtypeStruct((16, 320), f32),
            jax.ShapeDtypeStruct((320, 448), f32),
        ),
        in_specs=[pl.BlockSpec(memory_space=pltpu.SMEM)] + [anywhere] * 4 + [hbm] * 3,
        out_specs=(hbm,) * 3,
        scratch_shapes=[
            pltpu.VMEM((512, 512), bf16),
            pltpu.VMEM((512, 512), bf16),
            pltpu.VMEM((448, 512), bf16),
            pltpu.VMEM((448, 512), bf16),
            pltpu.VMEM((32, 40, 512), f32),
            pltpu.VMEM((448, 896), f32),
            pltpu.VMEM((320, 448), f32),
            pltpu.VMEM((896, 512), f32),
            pltpu.VMEM((512, 384), f32),
            pltpu.VMEM((16, 320), f32),
            pltpu.SemaphoreType.DMA((8,)),
            pltpu.SemaphoreType.DMA((4,)),
        ],
        compiler_params=pltpu.CompilerParams(vmem_limit_bytes=24 * 2**20),
        cost_estimate=pl.CostEstimate(flops=4 * 10**9, bytes_accessed=10**7, transcendentals=0),
        name="apply_inverse",
    )(column, high, low, d_high, d_low, *(keep(x, pltpu.HBM) for x in (gathered, trailing, rest)))


def per_device(diag_block, panel, trailing, truth_panel, truth_rest):
    rows, columns = ("x", "y"), ("z", "k")
    packed = pack(panel, truth_panel.T)
    gathered = lax.all_gather(packed, columns, axis=0, tiled=False)
    small = jnp.broadcast_to(diag_block.reshape(1, 4, 128), (32, 4, 128))
    pieces = lax.all_to_all(small, columns, 0, 0)
    strip = pieces.reshape(32, 4, 8, 16).transpose(1, 2, 0, 3).reshape(32, 512)
    whole = lax.all_to_all(copy_out(strip), rows, 0, 0).reshape(512, 512)
    copies, whole = lax.optimization_barrier((copy_out(panel), whole))
    dealt = lax.all_to_all(copies, rows, 0, 0)
    high, low = invert_factor(whole)
    column = (lax.axis_index("z") * 2 + lax.axis_index("k")).astype(jnp.int32)[None]
    d_high, d_low, factor = solve_dealt(high, low, dealt, panel)
    updated, solved, truth_updated = apply_inverse(
        column, high, low, d_high, d_low, gathered, trailing.T, truth_rest
    )
    return factor, updated.T, solved.T, truth_updated


def solution(mesh):
    fine = jax.sharding.Mesh(mesh.devices.reshape(4, 4, 16, 2), ("x", "y", "z", "k"))
    rows, columns = ("x", "y"), ("z", "k")
    tiled, whole = P(rows, columns), P(rows + columns, None)
    return jax.shard_map(
        per_device,
        mesh=fine,
        in_specs=(tiled, whole, tiled, tiled, tiled),
        out_specs=(whole, tiled, tiled, tiled),
        check_vma=False,
    )
```

```python
import jax
import jax.numpy as jnp
from jax import lax
from jax.experimental import pallas as pl
from jax.experimental.pallas import tpu as pltpu
from jax.sharding import PartitionSpec as P

HI = lax.Precision.HIGHEST
NT = (((1,), (1,)), ((), ()))
NN = (((1,), (0,)), ((), ()))


def halves(value):
    high = value.astype(jnp.bfloat16)
    return high, (value - high.astype(jnp.float32)).astype(jnp.bfloat16)


def factor_tile(d_ref, o_ref):
    n = 16
    lane = lax.broadcasted_iota(jnp.int32, (8, 128), 1)
    sub = lax.broadcasted_iota(jnp.int32, (8, 128), 0)
    full = lambda v: jnp.broadcast_to(v, (8, 128))
    m = [d_ref[8 * i:8 * i + 8, :] for i in range(n)]
    own = [full(m[0][:, c:c + 1]) for c in range(8)]
    for j in range(n):
        lo = 8 * j
        here = (lane >= lo) & (lane < lo + 8)
        s = {(a, c): full(own[c][a:a + 1, :]) for c in range(8) for a in range(c, 8)}
        rows = jnp.where(here, jnp.where(lane - lo == sub, 1.0, 0.0), m[j])
        r = [full(rows[a:a + 1, :]) for a in range(8)]
        if j + 1 < n:
            raw = [full(m[j + 1][:, lo + c:lo + c + 1]) for c in range(8)]
            own = [full(m[j + 1][:, lo + 8 + c:lo + 9 + c]) for c in range(8)]
            t = list(raw)
            near = jnp.where(here, 0.0, m[j + 1])
        l, inv, u = {}, [], []
        for c in range(8):
            q = lax.rsqrt(s[c, c])
            inv.append(q)
            for a in range(c + 1, 8):
                l[a, c] = s[a, c] * q
            for a in range(c + 1, 8):
                for b in range(c + 1, a + 1):
                    s[a, b] = s[a, b] - l[a, c] * l[b, c]
            u.append(r[c] * q)
            for a in range(c + 1, 8):
                r[a] = r[a] - l[a, c] * u[c]
            if j + 1 < n:
                t[c] = t[c] * q
                for a in range(c + 1, 8):
                    t[a] = t[a] - t[c] * l[a, c]
                for a in range(8):
                    own[a] = own[a] - t[c] * full(t[c][a:a + 1, :])
                near = near - t[c] * u[c]
        done = u[0]
        for a in range(1, 8):
            done = jnp.where(sub == a, u[a], done)
        o_ref[lo:lo + 8, :] = jnp.where(lane < lo + 8, done, 0.0)
        if j + 1 < n:
            m[j + 1] = near
        if j + 2 < n:
            v = [None] * 8
            for c in range(7, -1, -1):
                x = u[c]
                for a in range(7, c, -1):
                    x = x - l[a, c] * v[a]
                v[c] = x * inv[c]
            for i in range(j + 2, n):
                acc = jnp.where(here, 0.0, m[i])
                for c in range(8):
                    acc = acc - full(m[i][:, lo + c:lo + c + 1]) * v[c]
                m[i] = acc


def invert_kernel(a_hbm, inverse_hbm, m_ref, d_ref, t_ref, o_ref, sem):
    nb, n = 128, 512
    load = pltpu.make_async_copy(a_hbm, m_ref, sem.at[0])
    load.start()
    load.wait()
    dot = lambda p, q, dims: lax.dot_general(p, q, dims, precision=HI, preferred_element_type=jnp.float32)

    def after(k):
        lo, hi = k * nb, (k + 1) * nb
        t = t_ref[...]
        o_ref[lo:hi, lo:hi] = t
        if lo:
            o_ref[lo:hi, :lo] = dot(t, m_ref[lo:hi, :lo], NN)
        if hi < n:
            o_ref[lo:hi, hi:] = jnp.zeros((nb, n - hi), jnp.float32)
            left = dot(m_ref[hi:, lo:hi], t, NT)
            m_ref[hi:, hi:] = m_ref[hi:, hi:] - dot(left, left, NT)
            m_ref[hi:, lo:hi] = -dot(left, t, NN)
            if lo:
                m_ref[hi:, :lo] = m_ref[hi:, :lo] - dot(left, o_ref[lo:hi, :lo], NN)

    def step(k, carry):
        at = pl.ds(pl.multiple_of(k * nb, nb), nb)
        d_ref[...] = m_ref[at, at]
        factor_tile(d_ref, t_ref)
        for i in range(n // nb):
            pl.when(k == i)(lambda i=i: after(i))
        return carry

    lax.fori_loop(0, n // nb, step, 0)
    store = pltpu.make_async_copy(o_ref, inverse_hbm, sem.at[1])
    store.start()
    store.wait()


def invert_factor(block):
    n = block.shape[0]
    anywhere = pl.BlockSpec(memory_space=pl.ANY)
    return pl.pallas_call(
        invert_kernel,
        out_shape=jax.ShapeDtypeStruct((n, n), jnp.float32),
        in_specs=[anywhere],
        out_specs=anywhere,
        scratch_shapes=[
            pltpu.VMEM((n, n), jnp.float32),
            pltpu.VMEM((128, 128), jnp.float32),
            pltpu.VMEM((128, 128), jnp.float32),
            pltpu.VMEM((n, n), jnp.float32),
            pltpu.SemaphoreType.DMA((2,)),
        ],
        compiler_params=pltpu.CompilerParams(vmem_limit_bytes=16 * 2**20),
        cost_estimate=pl.CostEstimate(flops=10**10, bytes_accessed=2 * 10**6, transcendentals=0),
        name="invert_factor",
    )(block)


def pack_kernel(panel_hbm, truth_hbm, packed_hbm, panel, truth, packed, sem):
    first = pltpu.make_async_copy(panel_hbm, panel, sem.at[0])
    second = pltpu.make_async_copy(truth_hbm, truth, sem.at[1])
    first.start()
    second.start()
    second.wait()
    packed[28:32, :] = jnp.zeros((4, 512), jnp.float32)
    for q in range(4):
        packed[28:32, 128 * q:128 * q + 64] = truth[4 * q:4 * q + 4, 256:320]
    packed[32:40, 0:256] = truth[0:8, 0:256]
    packed[32:40, 256:512] = truth[8:16, 0:256]
    first.wait()
    packed[0:28, :] = panel[...]
    store = pltpu.make_async_copy(packed, packed_hbm, sem.at[2])
    store.start()
    store.wait()


def pack(panel, truth):
    f32 = jnp.float32
    hbm = pl.BlockSpec(memory_space=pltpu.HBM)
    keep = pltpu.with_memory_space_constraint
    return pl.pallas_call(
        pack_kernel,
        out_shape=jax.ShapeDtypeStruct((40, 512), f32),
        in_specs=[hbm, hbm],
        out_specs=hbm,
        scratch_shapes=[
            pltpu.VMEM((28, 512), f32),
            pltpu.VMEM((16, 320), f32),
            pltpu.VMEM((40, 512), f32),
            pltpu.SemaphoreType.DMA((3,)),
        ],
        compiler_params=pltpu.CompilerParams(vmem_limit_bytes=2 * 2**20),
        name="pack",
    )(keep(panel, pltpu.HBM), keep(truth, pltpu.HBM))


def copy_kernel(strip_ref, copies_hbm, sem):
    copies = [pltpu.make_async_copy(strip_ref, copies_hbm.at[i], sem.at[i]) for i in range(16)]
    for copy in copies:
        copy.start()
    for copy in copies:
        copy.wait()


def copy_out(strip):
    return pl.pallas_call(
        copy_kernel,
        out_shape=jax.ShapeDtypeStruct((16,) + strip.shape, strip.dtype),
        in_specs=[pl.BlockSpec(memory_space=pltpu.VMEM)],
        out_specs=pl.BlockSpec(memory_space=pl.ANY),
        scratch_shapes=[pltpu.SemaphoreType.DMA((16,))],
        compiler_params=pltpu.CompilerParams(vmem_limit_bytes=4 * 2**20),
        name="copy_out",
    )(strip)


def thrice(a, b, dims):
    dot = lambda p, q: lax.dot_general(p, q, dims, preferred_element_type=jnp.float32)
    return dot(a[0], b[0]) + dot(a[0], b[1]) + dot(a[1], b[0])


def dealt_kernel(inverse_any, dealt_any, panel_hbm, w_high_any, w_low_any, factor_hbm, inverse, dealt, stack, w_high, w_low, factor, sem):
    loads = [
        pltpu.make_async_copy(src, dst, sem.at[i])
        for i, (src, dst) in enumerate([(dealt_any, dealt), (panel_hbm, factor), (inverse_any, inverse)])
    ]
    for load in loads:
        load.start()
    loads[0].wait()
    loads[1].wait()
    for r in range(16):
        stack[28 * r:28 * r + 28, :] = dealt[r]
    stack[448:476, :] = factor[...]
    stack[476:480, :] = jnp.zeros((4, 512), jnp.float32)
    loads[2].wait()
    dot = lambda p, q, dims: lax.dot_general(p, q, dims, precision=HI, preferred_element_type=jnp.float32)
    left = dot(stack[:, :256], inverse[:256, :256], NT)
    right = dot(stack[...], inverse[256:, :], NT)
    factor[:, :256] = left[448:476, :]
    factor[:, 256:] = right[448:476, :]
    w_left = dot(left[:448], inverse[:256, :256], NN) + dot(right[:448], inverse[256:, :256], NN)
    w_right = dot(right[:448], inverse[256:, 256:], NN)
    w_high[:, :256], w_low[:, :256] = halves(w_left)
    w_high[:, 256:], w_low[:, 256:] = halves(w_right)
    stores = [
        pltpu.make_async_copy(src, dst, sem.at[3 + i])
        for i, (src, dst) in enumerate([(factor, factor_hbm), (w_high, w_high_any), (w_low, w_low_any)])
    ]
    for store in stores:
        store.start()
    for store in stores:
        store.wait()


def solve_dealt(inverse, dealt, panel):
    f32, bf16 = jnp.float32, jnp.bfloat16
    anywhere, hbm = pl.BlockSpec(memory_space=pl.ANY), pl.BlockSpec(memory_space=pltpu.HBM)
    half = jax.ShapeDtypeStruct((448, 512), bf16)
    return pl.pallas_call(
        dealt_kernel,
        out_shape=(half, half, jax.ShapeDtypeStruct((28, 512), f32)),
        in_specs=[anywhere] * 2 + [hbm],
        out_specs=(anywhere, anywhere, hbm),
        scratch_shapes=[
            pltpu.VMEM((512, 512), f32),
            pltpu.VMEM((16, 28, 512), f32),
            pltpu.VMEM((480, 512), f32),
            pltpu.VMEM((448, 512), bf16),
            pltpu.VMEM((448, 512), bf16),
            pltpu.VMEM((28, 512), f32),
            pltpu.SemaphoreType.DMA((6,)),
        ],
        compiler_params=pltpu.CompilerParams(vmem_limit_bytes=16 * 2**20),
        cost_estimate=pl.CostEstimate(flops=10**9, bytes_accessed=2 * 10**6, transcendentals=0),
        name="solve_dealt",
    )(inverse, dealt, pltpu.with_memory_space_constraint(panel, pltpu.HBM))


def apply_kernel(
    col_ref, inverse_any, w_high_any, w_low_any, gathered_hbm, trailing_hbm, rest_hbm,
    updated_hbm, solved_hbm, truth_hbm,
    own, w_high, w_low, gathered, trailing, rest, stack, truth, solved, sem, out_sem,
):
    at = pl.ds(pl.multiple_of(col_ref[0] * 16, 16), 16)
    loads = [
        pltpu.make_async_copy(src, dst, sem.at[i])
        for i, (src, dst) in enumerate(
            [
                (gathered_hbm.at[0:19], gathered.at[0:19]), (w_high_any, w_high), (w_low_any, w_low),
                (trailing_hbm, trailing), (gathered_hbm.at[19:32], gathered.at[19:32]),
                (inverse_any.at[at], own), (rest_hbm, rest),
            ]
        )
    ]
    for load in loads:
        load.start()
    stores = []

    def unpack(first, last):
        for c in range(first, last):
            stack[28 * c:28 * c + 28, :] = gathered[c, 0:28, :]
            truth[16 * c:16 * c + 8, 0:256] = gathered[c, 32:40, 0:256]
            truth[16 * c + 8:16 * c + 16, 0:256] = gathered[c, 32:40, 256:512]
            for q in range(4):
                truth[16 * c + 4 * q:16 * c + 4 * q + 4, 256:384] = gathered[c, 28:32, 128 * q:128 * q + 128]

    def put(src, dst):
        store = pltpu.make_async_copy(src, dst, out_sem.at[len(stores)])
        store.start()
        stores.append(store)

    def update(first, last):
        rows = halves(stack[first:last, :])
        trailing[:, first:last] = trailing[:, first:last] - thrice((w_high[...], w_low[...]), rows, NT)
        put(trailing.at[:, first:last], updated_hbm.at[:, first:last])

    loads[0].wait()
    unpack(0, 19)
    for load in loads[1:4]:
        load.wait()
    update(0, 512)
    loads[4].wait()
    unpack(19, 32)
    update(512, 896)
    columns = halves(truth[...].T[0:320, :])
    loads[5].wait()
    solved[...] = thrice(halves(own[...]), columns, NT)
    put(solved, solved_hbm)
    loads[6].wait()
    rest[...] = rest[...] - thrice(columns, (w_high[...], w_low[...]), NT)
    put(rest, truth_hbm)
    for store in stores:
        store.wait()


def apply_inverse(column, inverse, w_high, w_low, gathered, trailing, rest):
    f32, bf16 = jnp.float32, jnp.bfloat16
    anywhere, hbm = pl.BlockSpec(memory_space=pl.ANY), pl.BlockSpec(memory_space=pltpu.HBM)
    keep = pltpu.with_memory_space_constraint
    return pl.pallas_call(
        apply_kernel,
        out_shape=(
            jax.ShapeDtypeStruct((448, 896), f32),
            jax.ShapeDtypeStruct((16, 320), f32),
            jax.ShapeDtypeStruct((320, 448), f32),
        ),
        in_specs=[pl.BlockSpec(memory_space=pltpu.SMEM)] + [anywhere] * 3 + [hbm] * 3,
        out_specs=(hbm,) * 3,
        scratch_shapes=[
            pltpu.VMEM((16, 512), f32),
            pltpu.VMEM((448, 512), bf16),
            pltpu.VMEM((448, 512), bf16),
            pltpu.VMEM((32, 40, 512), f32),
            pltpu.VMEM((448, 896), f32),
            pltpu.VMEM((320, 448), f32),
            pltpu.VMEM((896, 512), f32),
            pltpu.VMEM((512, 384), f32),
            pltpu.VMEM((16, 320), f32),
            pltpu.SemaphoreType.DMA((7,)),
            pltpu.SemaphoreType.DMA((4,)),
        ],
        compiler_params=pltpu.CompilerParams(vmem_limit_bytes=24 * 2**20),
        cost_estimate=pl.CostEstimate(flops=4 * 10**9, bytes_accessed=10**7, transcendentals=0),
        name="apply_inverse",
    )(column, inverse, w_high, w_low, *(keep(x, pltpu.HBM) for x in (gathered, trailing, rest)))


def per_device(diag_block, panel, trailing, truth_panel, truth_rest):
    rows, columns = ("x", "y"), ("z", "k")
    packed = pack(panel, truth_panel.T)
    gathered = lax.all_gather(packed, columns, axis=0, tiled=False)
    small = jnp.broadcast_to(diag_block.reshape(1, 4, 128), (32, 4, 128))
    pieces = lax.all_to_all(small, columns, 0, 0)
    strip = pieces.reshape(32, 4, 8, 16).transpose(1, 2, 0, 3).reshape(32, 512)
    whole = lax.all_to_all(copy_out(strip), rows, 0, 0).reshape(512, 512)
    copies, whole = lax.optimization_barrier((copy_out(panel), whole))
    dealt = lax.all_to_all(copies, rows, 0, 0)
    inverse = invert_factor(whole)
    column = (lax.axis_index("z") * 2 + lax.axis_index("k")).astype(jnp.int32)[None]
    w_high, w_low, factor = solve_dealt(inverse, dealt, panel)
    updated, solved, truth_updated = apply_inverse(
        column, inverse, w_high, w_low, gathered, trailing.T, truth_rest
    )
    return factor, updated.T, solved.T, truth_updated


def solution(mesh):
    fine = jax.sharding.Mesh(mesh.devices.reshape(4, 4, 16, 2), ("x", "y", "z", "k"))
    rows, columns = ("x", "y"), ("z", "k")
    tiled, whole = P(rows, columns), P(rows + columns, None)
    return jax.shard_map(
        per_device,
        mesh=fine,
        in_specs=(tiled, whole, tiled, tiled, tiled),
        out_specs=(whole, tiled, tiled, tiled),
        check_vma=False,
    )
```

```python
import jax
import jax.numpy as jnp
from jax import lax
from jax.experimental import pallas as pl
from jax.experimental.pallas import tpu as pltpu
from jax.sharding import PartitionSpec as P

HI = lax.Precision.HIGHEST
NT = (((1,), (1,)), ((), ()))
NN = (((1,), (0,)), ((), ()))


def halves(value):
    high = value.astype(jnp.bfloat16)
    return high, (value - high.astype(jnp.float32)).astype(jnp.bfloat16)


def factor_tile(d_ref, o_ref):
    n = 16
    lane = lax.broadcasted_iota(jnp.int32, (8, 128), 1)
    sub = lax.broadcasted_iota(jnp.int32, (8, 128), 0)
    full = lambda v: jnp.broadcast_to(v, (8, 128))
    m = [d_ref[8 * i:8 * i + 8, :] for i in range(n)]
    own = [full(m[0][:, c:c + 1]) for c in range(8)]
    for j in range(n):
        lo = 8 * j
        here = (lane >= lo) & (lane < lo + 8)
        s = {(a, c): full(own[c][a:a + 1, :]) for c in range(8) for a in range(c, 8)}
        rows = jnp.where(here, jnp.where(lane - lo == sub, 1.0, 0.0), m[j])
        r = [full(rows[a:a + 1, :]) for a in range(8)]
        if j + 1 < n:
            raw = [full(m[j + 1][:, lo + c:lo + c + 1]) for c in range(8)]
            own = [full(m[j + 1][:, lo + 8 + c:lo + 9 + c]) for c in range(8)]
            t = list(raw)
            near = jnp.where(here, 0.0, m[j + 1])
        l, inv, u = {}, [], []
        for c in range(8):
            q = lax.rsqrt(s[c, c])
            inv.append(q)
            for a in range(c + 1, 8):
                l[a, c] = s[a, c] * q
            for a in range(c + 1, 8):
                for b in range(c + 1, a + 1):
                    s[a, b] = s[a, b] - l[a, c] * l[b, c]
            u.append(r[c] * q)
            for a in range(c + 1, 8):
                r[a] = r[a] - l[a, c] * u[c]
            if j + 1 < n:
                t[c] = t[c] * q
                for a in range(c + 1, 8):
                    t[a] = t[a] - t[c] * l[a, c]
                for a in range(8):
                    own[a] = own[a] - t[c] * full(t[c][a:a + 1, :])
                near = near - t[c] * u[c]
        done = u[0]
        for a in range(1, 8):
            done = jnp.where(sub == a, u[a], done)
        o_ref[lo:lo + 8, :] = jnp.where(lane < lo + 8, done, 0.0)
        if j + 1 < n:
            m[j + 1] = near
        if j + 2 < n:
            v = [None] * 8
            for c in range(7, -1, -1):
                x = u[c]
                for a in range(7, c, -1):
                    x = x - l[a, c] * v[a]
                v[c] = x * inv[c]
            for i in range(j + 2, n):
                acc = jnp.where(here, 0.0, m[i])
                for c in range(8):
                    acc = acc - full(m[i][:, lo + c:lo + c + 1]) * v[c]
                m[i] = acc


def invert_kernel(a_hbm, inverse_hbm, m_ref, d_ref, t_ref, o_ref, sem):
    nb, n = 128, 512
    load = pltpu.make_async_copy(a_hbm, m_ref, sem.at[0])
    load.start()
    load.wait()
    dot = lambda p, q, dims: lax.dot_general(p, q, dims, precision=HI, preferred_element_type=jnp.float32)

    def after(k):
        lo, hi = k * nb, (k + 1) * nb
        t = t_ref[...]
        o_ref[lo:hi, lo:hi] = t
        if lo:
            o_ref[lo:hi, :lo] = dot(t, m_ref[lo:hi, :lo], NN)
        if hi < n:
            o_ref[lo:hi, hi:] = jnp.zeros((nb, n - hi), jnp.float32)
            left = dot(m_ref[hi:, lo:hi], t, NT)
            m_ref[hi:, hi:] = m_ref[hi:, hi:] - dot(left, left, NT)
            m_ref[hi:, lo:hi] = -dot(left, t, NN)
            if lo:
                m_ref[hi:, :lo] = m_ref[hi:, :lo] - dot(left, o_ref[lo:hi, :lo], NN)

    def step(k, carry):
        at = pl.ds(pl.multiple_of(k * nb, nb), nb)
        d_ref[...] = m_ref[at, at]
        factor_tile(d_ref, t_ref)
        for i in range(n // nb):
            pl.when(k == i)(lambda i=i: after(i))
        return carry

    lax.fori_loop(0, n // nb, step, 0)
    store = pltpu.make_async_copy(o_ref, inverse_hbm, sem.at[1])
    store.start()
    store.wait()


def invert_factor(block):
    n = block.shape[0]
    anywhere = pl.BlockSpec(memory_space=pl.ANY)
    return pl.pallas_call(
        invert_kernel,
        out_shape=jax.ShapeDtypeStruct((n, n), jnp.float32),
        in_specs=[anywhere],
        out_specs=anywhere,
        scratch_shapes=[
            pltpu.VMEM((n, n), jnp.float32),
            pltpu.VMEM((128, 128), jnp.float32),
            pltpu.VMEM((128, 128), jnp.float32),
            pltpu.VMEM((n, n), jnp.float32),
            pltpu.SemaphoreType.DMA((2,)),
        ],
        compiler_params=pltpu.CompilerParams(vmem_limit_bytes=16 * 2**20),
        cost_estimate=pl.CostEstimate(flops=10**10, bytes_accessed=2 * 10**6, transcendentals=0),
        name="invert_factor",
    )(block)


def pack_kernel(panel_hbm, truth_hbm, packed_hbm, panel, truth, packed, sem):
    first = pltpu.make_async_copy(panel_hbm, panel, sem.at[0])
    second = pltpu.make_async_copy(truth_hbm, truth, sem.at[1])
    first.start()
    second.start()
    second.wait()
    packed[28:32, :] = jnp.zeros((4, 512), jnp.float32)
    for q in range(4):
        packed[28:32, 128 * q:128 * q + 64] = truth[4 * q:4 * q + 4, 256:320]
    packed[32:40, 0:256] = truth[0:8, 0:256]
    packed[32:40, 256:512] = truth[8:16, 0:256]
    first.wait()
    packed[0:28, :] = panel[...]
    store = pltpu.make_async_copy(packed, packed_hbm, sem.at[2])
    store.start()
    store.wait()


def pack(panel, truth):
    f32 = jnp.float32
    hbm = pl.BlockSpec(memory_space=pltpu.HBM)
    keep = pltpu.with_memory_space_constraint
    return pl.pallas_call(
        pack_kernel,
        out_shape=jax.ShapeDtypeStruct((40, 512), f32),
        in_specs=[hbm, hbm],
        out_specs=hbm,
        scratch_shapes=[
            pltpu.VMEM((28, 512), f32),
            pltpu.VMEM((16, 320), f32),
            pltpu.VMEM((40, 512), f32),
            pltpu.SemaphoreType.DMA((3,)),
        ],
        compiler_params=pltpu.CompilerParams(vmem_limit_bytes=2 * 2**20),
        name="pack",
    )(keep(panel, pltpu.HBM), keep(truth, pltpu.HBM))


def copy_kernel(strip_ref, copies_hbm, sem):
    copies = [pltpu.make_async_copy(strip_ref, copies_hbm.at[i], sem.at[i]) for i in range(16)]
    for copy in copies:
        copy.start()
    for copy in copies:
        copy.wait()


def copy_out(strip):
    return pl.pallas_call(
        copy_kernel,
        out_shape=jax.ShapeDtypeStruct((16,) + strip.shape, strip.dtype),
        in_specs=[pl.BlockSpec(memory_space=pltpu.VMEM)],
        out_specs=pl.BlockSpec(memory_space=pl.ANY),
        scratch_shapes=[pltpu.SemaphoreType.DMA((16,))],
        compiler_params=pltpu.CompilerParams(vmem_limit_bytes=4 * 2**20),
        name="copy_out",
    )(strip)


def thrice(a, b, dims):
    dot = lambda p, q: lax.dot_general(p, q, dims, preferred_element_type=jnp.float32)
    return dot(a[0], b[0]) + dot(a[0], b[1]) + dot(a[1], b[0])


def dealt_kernel(inverse_any, dealt_any, panel_hbm, w_high_any, w_low_any, factor_hbm, inverse, dealt, stack, w_high, w_low, factor, sem):
    loads = [
        pltpu.make_async_copy(src, dst, sem.at[i])
        for i, (src, dst) in enumerate([(dealt_any, dealt), (panel_hbm, factor), (inverse_any, inverse)])
    ]
    for load in loads:
        load.start()
    loads[0].wait()
    loads[1].wait()
    for r in range(16):
        stack[28 * r:28 * r + 28, :] = dealt[r]
    stack[448:476, :] = factor[...]
    stack[476:480, :] = jnp.zeros((4, 512), jnp.float32)
    loads[2].wait()
    dot = lambda p, q, dims: lax.dot_general(p, q, dims, precision=HI, preferred_element_type=jnp.float32)
    left = dot(stack[:, :256], inverse[:256, :256], NT)
    right = dot(stack[...], inverse[256:, :], NT)
    factor[:, :256] = left[448:476, :]
    factor[:, 256:] = right[448:476, :]
    w_left = dot(left[:448], inverse[:256, :256], NN) + dot(right[:448], inverse[256:, :256], NN)
    w_right = dot(right[:448], inverse[256:, 256:], NN)
    w_high[:, :256], w_low[:, :256] = halves(w_left)
    w_high[:, 256:], w_low[:, 256:] = halves(w_right)
    stores = [
        pltpu.make_async_copy(src, dst, sem.at[3 + i])
        for i, (src, dst) in enumerate([(factor, factor_hbm), (w_high, w_high_any), (w_low, w_low_any)])
    ]
    for store in stores:
        store.start()
    for store in stores:
        store.wait()


def solve_dealt(inverse, dealt, panel):
    f32, bf16 = jnp.float32, jnp.bfloat16
    anywhere, hbm = pl.BlockSpec(memory_space=pl.ANY), pl.BlockSpec(memory_space=pltpu.HBM)
    half = jax.ShapeDtypeStruct((448, 512), bf16)
    return pl.pallas_call(
        dealt_kernel,
        out_shape=(half, half, jax.ShapeDtypeStruct((28, 512), f32)),
        in_specs=[anywhere] * 2 + [hbm],
        out_specs=(anywhere, anywhere, hbm),
        scratch_shapes=[
            pltpu.VMEM((512, 512), f32),
            pltpu.VMEM((16, 28, 512), f32),
            pltpu.VMEM((480, 512), f32),
            pltpu.VMEM((448, 512), bf16),
            pltpu.VMEM((448, 512), bf16),
            pltpu.VMEM((28, 512), f32),
            pltpu.SemaphoreType.DMA((6,)),
        ],
        compiler_params=pltpu.CompilerParams(vmem_limit_bytes=16 * 2**20),
        cost_estimate=pl.CostEstimate(flops=10**9, bytes_accessed=2 * 10**6, transcendentals=0),
        name="solve_dealt",
    )(inverse, dealt, pltpu.with_memory_space_constraint(panel, pltpu.HBM))


def apply_kernel(
    col_ref, inverse_any, w_high_any, w_low_any, gathered_hbm, trailing_hbm, rest_hbm,
    updated_hbm, solved_hbm, truth_hbm,
    own, w_high, w_low, gathered, trailing, rest, stack, truth, solved, sem, out_sem,
):
    at = pl.ds(pl.multiple_of(col_ref[0] * 16, 16), 16)
    pieces = ((0, 10), (10, 19), (19, 28), (28, 32))
    loads = [
        pltpu.make_async_copy(src, dst, sem.at[i])
        for i, (src, dst) in enumerate(
            [(gathered_hbm.at[a:b], gathered.at[a:b]) for a, b in pieces]
            + [
                (w_high_any, w_high), (w_low_any, w_low), (trailing_hbm, trailing),
                (inverse_any.at[at], own), (rest_hbm, rest),
            ]
        )
    ]
    stores = []

    def unpack(first, last):
        for c in range(first, last):
            stack[28 * c:28 * c + 28, :] = gathered[c, 0:28, :]
            truth[16 * c:16 * c + 8, 0:256] = gathered[c, 32:40, 0:256]
            truth[16 * c + 8:16 * c + 16, 0:256] = gathered[c, 32:40, 256:512]
            for q in range(4):
                truth[16 * c + 4 * q:16 * c + 4 * q + 4, 256:384] = gathered[c, 28:32, 128 * q:128 * q + 128]

    def put(src, dst):
        store = pltpu.make_async_copy(src, dst, out_sem.at[len(stores)])
        store.start()
        stores.append(store)

    def product(first, last):
        return thrice((w_high[...], w_low[...]), halves(stack[first:last, :]), NT)

    def finish(first, last, value):
        trailing[:, first:last] = trailing[:, first:last] - value
        put(trailing.at[:, first:last], updated_hbm.at[:, first:last])

    for i in (0, 4, 5, 1):
        loads[i].start()
    loads[0].wait()
    for i in (6, 2, 3, 7, 8):
        loads[i].start()
    unpack(0, 10)
    for i in (4, 5, 1):
        loads[i].wait()
    unpack(10, 19)
    value = product(0, 256)
    for i in (6, 2):
        loads[i].wait()
    finish(0, 256, value)
    unpack(19, 28)
    value = product(256, 512)
    for i in (3, 7, 8):
        loads[i].wait()
    finish(256, 512, value)
    unpack(28, 32)
    finish(512, 768, product(512, 768))
    columns = halves(truth[...].T[0:320, :])
    rest[...] = rest[...] - thrice(columns, (w_high[...], w_low[...]), NT)
    put(rest, truth_hbm)
    solved[...] = thrice(halves(own[...]), columns, NT)
    put(solved, solved_hbm)
    finish(768, 896, product(768, 896))
    for store in stores:
        store.wait()


def apply_inverse(column, inverse, w_high, w_low, gathered, trailing, rest):
    f32, bf16 = jnp.float32, jnp.bfloat16
    anywhere, hbm = pl.BlockSpec(memory_space=pl.ANY), pl.BlockSpec(memory_space=pltpu.HBM)
    keep = pltpu.with_memory_space_constraint
    return pl.pallas_call(
        apply_kernel,
        out_shape=(
            jax.ShapeDtypeStruct((448, 896), f32),
            jax.ShapeDtypeStruct((16, 320), f32),
            jax.ShapeDtypeStruct((320, 448), f32),
        ),
        in_specs=[pl.BlockSpec(memory_space=pltpu.SMEM)] + [anywhere] * 3 + [hbm] * 3,
        out_specs=(hbm,) * 3,
        scratch_shapes=[
            pltpu.VMEM((16, 512), f32),
            pltpu.VMEM((448, 512), bf16),
            pltpu.VMEM((448, 512), bf16),
            pltpu.VMEM((32, 40, 512), f32),
            pltpu.VMEM((448, 896), f32),
            pltpu.VMEM((320, 448), f32),
            pltpu.VMEM((896, 512), f32),
            pltpu.VMEM((512, 384), f32),
            pltpu.VMEM((16, 320), f32),
            pltpu.SemaphoreType.DMA((9,)),
            pltpu.SemaphoreType.DMA((6,)),
        ],
        compiler_params=pltpu.CompilerParams(vmem_limit_bytes=24 * 2**20),
        cost_estimate=pl.CostEstimate(flops=4 * 10**9, bytes_accessed=10**7, transcendentals=0),
        name="apply_inverse",
    )(column, inverse, w_high, w_low, *(keep(x, pltpu.HBM) for x in (gathered, trailing, rest)))


def per_device(diag_block, panel, trailing, truth_panel, truth_rest):
    rows, columns = ("x", "y"), ("z", "k")
    packed = pack(panel, truth_panel.T)
    gathered = lax.all_gather(packed, columns, axis=0, tiled=False)
    small = jnp.broadcast_to(diag_block.reshape(1, 4, 128), (32, 4, 128))
    pieces = lax.all_to_all(small, columns, 0, 0)
    strip = pieces.reshape(32, 4, 8, 16).transpose(1, 2, 0, 3).reshape(32, 512)
    whole = lax.all_to_all(copy_out(strip), rows, 0, 0).reshape(512, 512)
    copies, whole = lax.optimization_barrier((copy_out(panel), whole))
    dealt = lax.all_to_all(copies, rows, 0, 0)
    inverse = invert_factor(whole)
    column = (lax.axis_index("z") * 2 + lax.axis_index("k")).astype(jnp.int32)[None]
    w_high, w_low, factor = solve_dealt(inverse, dealt, panel)
    updated, solved, truth_updated = apply_inverse(
        column, inverse, w_high, w_low, gathered, trailing.T, truth_rest
    )
    return factor, updated.T, solved.T, truth_updated


def solution(mesh):
    fine = jax.sharding.Mesh(mesh.devices.reshape(4, 4, 16, 2), ("x", "y", "z", "k"))
    rows, columns = ("x", "y"), ("z", "k")
    tiled, whole = P(rows, columns), P(rows + columns, None)
    return jax.shard_map(
        per_device,
        mesh=fine,
        in_specs=(tiled, whole, tiled, tiled, tiled),
        out_specs=(whole, tiled, tiled, tiled),
        check_vma=False,
    )
```

```python
import jax
import jax.numpy as jnp
from jax import lax
from jax.experimental import pallas as pl
from jax.experimental.pallas import tpu as pltpu
from jax.sharding import PartitionSpec as P

HI = lax.Precision.HIGHEST
NT = (((1,), (1,)), ((), ()))
NN = (((1,), (0,)), ((), ()))


def halves(value):
    high = value.astype(jnp.bfloat16)
    return high, (value - high.astype(jnp.float32)).astype(jnp.bfloat16)


def factor_tile(d_ref, o_ref):
    n = 16
    lane = lax.broadcasted_iota(jnp.int32, (8, 128), 1)
    sub = lax.broadcasted_iota(jnp.int32, (8, 128), 0)
    full = lambda v: jnp.broadcast_to(v, (8, 128))
    m = [d_ref[8 * i:8 * i + 8, :] for i in range(n)]
    own = [full(m[0][:, c:c + 1]) for c in range(8)]
    for j in range(n):
        lo = 8 * j
        here = (lane >= lo) & (lane < lo + 8)
        s = {(a, c): full(own[c][a:a + 1, :]) for c in range(8) for a in range(c, 8)}
        rows = jnp.where(here, jnp.where(lane - lo == sub, 1.0, 0.0), m[j])
        r = [full(rows[a:a + 1, :]) for a in range(8)]
        if j + 1 < n:
            raw = [full(m[j + 1][:, lo + c:lo + c + 1]) for c in range(8)]
            own = [full(m[j + 1][:, lo + 8 + c:lo + 9 + c]) for c in range(8)]
            t = list(raw)
            near = jnp.where(here, 0.0, m[j + 1])
        l, inv, u = {}, [], []
        for c in range(8):
            q = lax.rsqrt(s[c, c])
            inv.append(q)
            for a in range(c + 1, 8):
                l[a, c] = s[a, c] * q
            for a in range(c + 1, 8):
                for b in range(c + 1, a + 1):
                    s[a, b] = s[a, b] - l[a, c] * l[b, c]
            u.append(r[c] * q)
            for a in range(c + 1, 8):
                r[a] = r[a] - l[a, c] * u[c]
            if j + 1 < n:
                t[c] = t[c] * q
                for a in range(c + 1, 8):
                    t[a] = t[a] - t[c] * l[a, c]
                for a in range(8):
                    own[a] = own[a] - t[c] * full(t[c][a:a + 1, :])
                near = near - t[c] * u[c]
        done = u[0]
        for a in range(1, 8):
            done = jnp.where(sub == a, u[a], done)
        o_ref[lo:lo + 8, :] = jnp.where(lane < lo + 8, done, 0.0)
        if j + 1 < n:
            m[j + 1] = near
        if j + 2 < n:
            v = [None] * 8
            for c in range(7, -1, -1):
                x = u[c]
                for a in range(7, c, -1):
                    x = x - l[a, c] * v[a]
                v[c] = x * inv[c]
            for i in range(j + 2, n):
                acc = jnp.where(here, 0.0, m[i])
                for c in range(8):
                    acc = acc - full(m[i][:, lo + c:lo + c + 1]) * v[c]
                m[i] = acc


def invert_kernel(a_hbm, inverse_hbm, m_ref, d_ref, t_ref, o_ref, sem):
    nb, n = 128, 512
    load = pltpu.make_async_copy(a_hbm, m_ref, sem.at[0])
    load.start()
    load.wait()
    dot = lambda p, q, dims: lax.dot_general(p, q, dims, precision=HI, preferred_element_type=jnp.float32)

    def after(k):
        lo, hi = k * nb, (k + 1) * nb
        t = t_ref[...]
        o_ref[lo:hi, lo:hi] = t
        if lo:
            o_ref[lo:hi, :lo] = dot(t, m_ref[lo:hi, :lo], NN)
        if hi < n:
            o_ref[lo:hi, hi:] = jnp.zeros((nb, n - hi), jnp.float32)
            left = dot(m_ref[hi:, lo:hi], t, NT)
            m_ref[hi:, hi:] = m_ref[hi:, hi:] - dot(left, left, NT)
            m_ref[hi:, lo:hi] = -dot(left, t, NN)
            if lo:
                m_ref[hi:, :lo] = m_ref[hi:, :lo] - dot(left, o_ref[lo:hi, :lo], NN)

    def step(k, carry):
        at = pl.ds(pl.multiple_of(k * nb, nb), nb)
        d_ref[...] = m_ref[at, at]
        factor_tile(d_ref, t_ref)
        for i in range(n // nb):
            pl.when(k == i)(lambda i=i: after(i))
        return carry

    lax.fori_loop(0, n // nb, step, 0)
    store = pltpu.make_async_copy(o_ref, inverse_hbm, sem.at[1])
    store.start()
    store.wait()


def invert_factor(block):
    n = block.shape[0]
    anywhere = pl.BlockSpec(memory_space=pl.ANY)
    return pl.pallas_call(
        invert_kernel,
        out_shape=jax.ShapeDtypeStruct((n, n), jnp.float32),
        in_specs=[anywhere],
        out_specs=anywhere,
        scratch_shapes=[
            pltpu.VMEM((n, n), jnp.float32),
            pltpu.VMEM((128, 128), jnp.float32),
            pltpu.VMEM((128, 128), jnp.float32),
            pltpu.VMEM((n, n), jnp.float32),
            pltpu.SemaphoreType.DMA((2,)),
        ],
        compiler_params=pltpu.CompilerParams(vmem_limit_bytes=16 * 2**20),
        cost_estimate=pl.CostEstimate(flops=10**10, bytes_accessed=2 * 10**6, transcendentals=0),
        name="invert_factor",
    )(block)


def pack_kernel(panel_hbm, truth_hbm, packed_hbm, panel, truth, packed, sem):
    first = pltpu.make_async_copy(panel_hbm, panel, sem.at[0])
    second = pltpu.make_async_copy(truth_hbm, truth, sem.at[1])
    first.start()
    second.start()
    second.wait()
    packed[28:32, :] = jnp.zeros((4, 512), jnp.float32)
    for q in range(4):
        packed[28:32, 128 * q:128 * q + 64] = truth[4 * q:4 * q + 4, 256:320]
    packed[32:40, 0:256] = truth[0:8, 0:256]
    packed[32:40, 256:512] = truth[8:16, 0:256]
    first.wait()
    packed[0:28, :] = panel[...]
    store = pltpu.make_async_copy(packed, packed_hbm, sem.at[2])
    store.start()
    store.wait()


def pack(panel, truth):
    f32 = jnp.float32
    hbm = pl.BlockSpec(memory_space=pltpu.HBM)
    keep = pltpu.with_memory_space_constraint
    return pl.pallas_call(
        pack_kernel,
        out_shape=jax.ShapeDtypeStruct((40, 512), f32),
        in_specs=[hbm, hbm],
        out_specs=hbm,
        scratch_shapes=[
            pltpu.VMEM((28, 512), f32),
            pltpu.VMEM((16, 320), f32),
            pltpu.VMEM((40, 512), f32),
            pltpu.SemaphoreType.DMA((3,)),
        ],
        compiler_params=pltpu.CompilerParams(vmem_limit_bytes=2 * 2**20),
        name="pack",
    )(keep(panel, pltpu.HBM), keep(truth, pltpu.HBM))


def copy_kernel(strip_ref, copies_hbm, sem):
    copies = [pltpu.make_async_copy(strip_ref, copies_hbm.at[i], sem.at[i]) for i in range(16)]
    for copy in copies:
        copy.start()
    for copy in copies:
        copy.wait()


def copy_out(strip):
    return pl.pallas_call(
        copy_kernel,
        out_shape=jax.ShapeDtypeStruct((16,) + strip.shape, strip.dtype),
        in_specs=[pl.BlockSpec(memory_space=pltpu.VMEM)],
        out_specs=pl.BlockSpec(memory_space=pl.ANY),
        scratch_shapes=[pltpu.SemaphoreType.DMA((16,))],
        compiler_params=pltpu.CompilerParams(vmem_limit_bytes=4 * 2**20),
        name="copy_out",
    )(strip)


def thrice(a, b, dims):
    dot = lambda p, q: lax.dot_general(p, q, dims, preferred_element_type=jnp.float32)
    return dot(a[0], b[0]) + dot(a[0], b[1]) + dot(a[1], b[0])


def dealt_kernel(inverse_any, dealt_any, panel_hbm, w_high, w_low, factor_hbm, inverse, dealt, stack, factor, sem):
    loads = [
        pltpu.make_async_copy(src, dst, sem.at[i])
        for i, (src, dst) in enumerate([(dealt_any, dealt), (panel_hbm, factor), (inverse_any, inverse)])
    ]
    for load in loads:
        load.start()
    loads[0].wait()
    loads[1].wait()
    for r in range(16):
        stack[28 * r:28 * r + 28, :] = dealt[r]
    stack[448:476, :] = factor[...]
    stack[476:480, :] = jnp.zeros((4, 512), jnp.float32)
    loads[2].wait()
    dot = lambda p, q, dims: lax.dot_general(p, q, dims, precision=HI, preferred_element_type=jnp.float32)
    left = dot(stack[:, :256], inverse[:256, :256], NT)
    right = dot(stack[...], inverse[256:, :], NT)
    factor[:, :256] = left[448:476, :]
    factor[:, 256:] = right[448:476, :]
    w_left = dot(left[:448], inverse[:256, :256], NN) + dot(right[:448], inverse[256:, :256], NN)
    w_right = dot(right[:448], inverse[256:, 256:], NN)
    w_high[:, :256], w_low[:, :256] = halves(w_left)
    w_high[:, 256:], w_low[:, 256:] = halves(w_right)
    store = pltpu.make_async_copy(factor, factor_hbm, sem.at[3])
    store.start()
    store.wait()


def solve_dealt(inverse, dealt, panel):
    f32, bf16 = jnp.float32, jnp.bfloat16
    anywhere, hbm = pl.BlockSpec(memory_space=pl.ANY), pl.BlockSpec(memory_space=pltpu.HBM)
    half = pltpu.VMEM((448, 512), bf16)
    vmem = pl.BlockSpec(memory_space=pltpu.VMEM)
    return pl.pallas_call(
        dealt_kernel,
        out_shape=(half, half, jax.ShapeDtypeStruct((28, 512), f32)),
        in_specs=[anywhere] * 2 + [hbm],
        out_specs=(vmem, vmem, hbm),
        scratch_shapes=[
            pltpu.VMEM((512, 512), f32),
            pltpu.VMEM((16, 28, 512), f32),
            pltpu.VMEM((480, 512), f32),
            pltpu.VMEM((28, 512), f32),
            pltpu.SemaphoreType.DMA((4,)),
        ],
        compiler_params=pltpu.CompilerParams(vmem_limit_bytes=16 * 2**20),
        cost_estimate=pl.CostEstimate(flops=10**9, bytes_accessed=2 * 10**6, transcendentals=0),
        name="solve_dealt",
    )(inverse, dealt, pltpu.with_memory_space_constraint(panel, pltpu.HBM))


def apply_kernel(
    col_ref, inverse_any, w_high, w_low, gathered_hbm, trailing_hbm, rest_hbm,
    updated_hbm, solved_hbm, truth_hbm,
    own, gathered, trailing, rest, stack, truth, solved, sem, out_sem,
):
    at = pl.ds(pl.multiple_of(col_ref[0] * 16, 16), 16)
    pieces = ((0, 10), (10, 19), (19, 28), (28, 32))
    loads = [
        pltpu.make_async_copy(src, dst, sem.at[i])
        for i, (src, dst) in enumerate(
            [(gathered_hbm.at[a:b], gathered.at[a:b]) for a, b in pieces]
            + [
                (trailing_hbm, trailing),
                (inverse_any.at[at], own), (rest_hbm, rest),
            ]
        )
    ]
    stores = []

    def unpack(first, last):
        for c in range(first, last):
            stack[28 * c:28 * c + 28, :] = gathered[c, 0:28, :]
            truth[16 * c:16 * c + 8, 0:256] = gathered[c, 32:40, 0:256]
            truth[16 * c + 8:16 * c + 16, 0:256] = gathered[c, 32:40, 256:512]
            for q in range(4):
                truth[16 * c + 4 * q:16 * c + 4 * q + 4, 256:384] = gathered[c, 28:32, 128 * q:128 * q + 128]

    def put(src, dst):
        store = pltpu.make_async_copy(src, dst, out_sem.at[len(stores)])
        store.start()
        stores.append(store)

    def product(first, last):
        high, low = halves(stack[first:last, :])
        dot = lambda p, q: lax.dot_general(p, q, NT, preferred_element_type=jnp.float32)
        both = dot(jnp.concatenate([w_high[...], w_low[...]], 0), high)
        return both[:448] + both[448:] + dot(w_high[...], low)

    def finish(first, last, value):
        trailing[:, first:last] = trailing[:, first:last] - value

    def send(first, last):
        put(trailing.at[:, first:last], updated_hbm.at[:, first:last])

    for i in (0, 1):
        loads[i].start()
    loads[0].wait()
    for i in (4, 2, 3, 5, 6):
        loads[i].start()
    unpack(0, 10)
    loads[1].wait()
    value = product(0, 256)
    unpack(10, 19)
    for i in (4, 2, 3, 5, 6):
        loads[i].wait()
    finish(0, 256, value)
    value = product(256, 512)
    unpack(19, 32)
    columns = halves(truth[...].T[0:320, :])
    finish(256, 512, value)
    value = product(512, 768)
    send(0, 256)
    send(256, 512)
    finish(512, 768, value)
    rest[...] = rest[...] - thrice(columns, (w_high[...], w_low[...]), NT)
    solved[...] = thrice(halves(own[...]), columns, NT)
    value = product(768, 896)
    send(512, 768)
    put(rest, truth_hbm)
    put(solved, solved_hbm)
    finish(768, 896, value)
    send(768, 896)
    for store in stores:
        store.wait()


def apply_inverse(column, inverse, w_high, w_low, gathered, trailing, rest):
    f32, bf16 = jnp.float32, jnp.bfloat16
    anywhere, hbm = pl.BlockSpec(memory_space=pl.ANY), pl.BlockSpec(memory_space=pltpu.HBM)
    keep = pltpu.with_memory_space_constraint
    return pl.pallas_call(
        apply_kernel,
        out_shape=(
            jax.ShapeDtypeStruct((448, 896), f32),
            jax.ShapeDtypeStruct((16, 320), f32),
            jax.ShapeDtypeStruct((320, 448), f32),
        ),
        in_specs=[pl.BlockSpec(memory_space=pltpu.SMEM), anywhere] + [pl.BlockSpec(memory_space=pltpu.VMEM)] * 2 + [hbm] * 3,
        out_specs=(hbm,) * 3,
        scratch_shapes=[
            pltpu.VMEM((16, 512), f32),
            pltpu.VMEM((32, 40, 512), f32),
            pltpu.VMEM((448, 896), f32),
            pltpu.VMEM((320, 448), f32),
            pltpu.VMEM((896, 512), f32),
            pltpu.VMEM((512, 384), f32),
            pltpu.VMEM((16, 320), f32),
            pltpu.SemaphoreType.DMA((7,)),
            pltpu.SemaphoreType.DMA((6,)),
        ],
        compiler_params=pltpu.CompilerParams(vmem_limit_bytes=24 * 2**20),
        cost_estimate=pl.CostEstimate(flops=4 * 10**9, bytes_accessed=10**7, transcendentals=0),
        name="apply_inverse",
    )(column, inverse, keep(w_high, pltpu.VMEM), keep(w_low, pltpu.VMEM), *(keep(x, pltpu.HBM) for x in (gathered, trailing, rest)))


def per_device(diag_block, panel, trailing, truth_panel, truth_rest):
    rows, columns = ("x", "y"), ("z", "k")
    packed = pack(panel, truth_panel.T)
    gathered = lax.all_gather(packed, columns, axis=0, tiled=False)
    small = jnp.broadcast_to(diag_block.reshape(1, 4, 128), (32, 4, 128))
    pieces = lax.all_to_all(small, columns, 0, 0)
    strip = pieces.reshape(32, 4, 8, 16).transpose(1, 2, 0, 3).reshape(32, 512)
    whole = lax.all_to_all(copy_out(strip), rows, 0, 0).reshape(512, 512)
    copies, whole = lax.optimization_barrier((copy_out(panel), whole))
    dealt = lax.all_to_all(copies, rows, 0, 0)
    inverse = invert_factor(whole)
    column = (lax.axis_index("z") * 2 + lax.axis_index("k")).astype(jnp.int32)[None]
    w_high, w_low, factor = solve_dealt(inverse, dealt, panel)
    updated, solved, truth_updated = apply_inverse(
        column, inverse, w_high, w_low, gathered, trailing.T, truth_rest
    )
    return factor, updated.T, solved.T, truth_updated


def solution(mesh):
    fine = jax.sharding.Mesh(mesh.devices.reshape(4, 4, 16, 2), ("x", "y", "z", "k"))
    rows, columns = ("x", "y"), ("z", "k")
    tiled, whole = P(rows, columns), P(rows + columns, None)
    return jax.shard_map(
        per_device,
        mesh=fine,
        in_specs=(tiled, whole, tiled, tiled, tiled),
        out_specs=(whole, tiled, tiled, tiled),
        check_vma=False,
    )
```

```python
import jax
import jax.numpy as jnp
from jax import lax
from jax.experimental import pallas as pl
from jax.experimental.pallas import tpu as pltpu
from jax.sharding import PartitionSpec as P

HI = lax.Precision.HIGHEST
NT = (((1,), (1,)), ((), ()))
NN = (((1,), (0,)), ((), ()))


def halves(value):
    high = value.astype(jnp.bfloat16)
    return high, (value - high.astype(jnp.float32)).astype(jnp.bfloat16)


def factor_tile(d_ref, o_ref):
    n = 16
    lane = lax.broadcasted_iota(jnp.int32, (8, 128), 1)
    sub = lax.broadcasted_iota(jnp.int32, (8, 128), 0)
    full = lambda v: jnp.broadcast_to(v, (8, 128))
    m = [d_ref[8 * i:8 * i + 8, :] for i in range(n)]
    own = [full(m[0][:, c:c + 1]) for c in range(8)]
    for j in range(n):
        lo = 8 * j
        here = (lane >= lo) & (lane < lo + 8)
        s = {(a, c): full(own[c][a:a + 1, :]) for c in range(8) for a in range(c, 8)}
        rows = jnp.where(here, jnp.where(lane - lo == sub, 1.0, 0.0), m[j])
        r = [full(rows[a:a + 1, :]) for a in range(8)]
        if j + 1 < n:
            raw = [full(m[j + 1][:, lo + c:lo + c + 1]) for c in range(8)]
            own = [full(m[j + 1][:, lo + 8 + c:lo + 9 + c]) for c in range(8)]
            t = list(raw)
            near = jnp.where(here, 0.0, m[j + 1])
        l, inv, u = {}, [], []
        for c in range(8):
            q = lax.rsqrt(s[c, c])
            inv.append(q)
            for a in range(c + 1, 8):
                l[a, c] = s[a, c] * q
            for a in range(c + 1, 8):
                for b in range(c + 1, a + 1):
                    s[a, b] = s[a, b] - l[a, c] * l[b, c]
            u.append(r[c] * q)
            for a in range(c + 1, 8):
                r[a] = r[a] - l[a, c] * u[c]
            if j + 1 < n:
                t[c] = t[c] * q
                for a in range(c + 1, 8):
                    t[a] = t[a] - t[c] * l[a, c]
                for a in range(8):
                    own[a] = own[a] - t[c] * full(t[c][a:a + 1, :])
                near = near - t[c] * u[c]
        done = u[0]
        for a in range(1, 8):
            done = jnp.where(sub == a, u[a], done)
        o_ref[lo:lo + 8, :] = jnp.where(lane < lo + 8, done, 0.0)
        if j + 1 < n:
            m[j + 1] = near
        if j + 2 < n:
            v = [None] * 8
            for c in range(7, -1, -1):
                x = u[c]
                for a in range(7, c, -1):
                    x = x - l[a, c] * v[a]
                v[c] = x * inv[c]
            for i in range(j + 2, n):
                acc = jnp.where(here, 0.0, m[i])
                for c in range(8):
                    acc = acc - full(m[i][:, lo + c:lo + c + 1]) * v[c]
                m[i] = acc


def invert_kernel(a_hbm, inverse_hbm, m_ref, d_ref, t_ref, o_ref, sem):
    nb, n = 128, 512
    load = pltpu.make_async_copy(a_hbm, m_ref, sem.at[0])
    load.start()
    load.wait()
    dot = lambda p, q, dims: lax.dot_general(p, q, dims, precision=HI, preferred_element_type=jnp.float32)

    def after(k):
        lo, hi = k * nb, (k + 1) * nb
        t = t_ref[...]
        o_ref[lo:hi, lo:hi] = t
        if lo:
            o_ref[lo:hi, :lo] = dot(t, m_ref[lo:hi, :lo], NN)
        if hi < n:
            o_ref[lo:hi, hi:] = jnp.zeros((nb, n - hi), jnp.float32)
            left = dot(m_ref[hi:, lo:hi], t, NT)
            m_ref[hi:, hi:] = m_ref[hi:, hi:] - dot(left, left, NT)
            m_ref[hi:, lo:hi] = -dot(left, t, NN)
            if lo:
                m_ref[hi:, :lo] = m_ref[hi:, :lo] - dot(left, o_ref[lo:hi, :lo], NN)

    def step(k, carry):
        at = pl.ds(pl.multiple_of(k * nb, nb), nb)
        d_ref[...] = m_ref[at, at]
        factor_tile(d_ref, t_ref)
        for i in range(n // nb):
            pl.when(k == i)(lambda i=i: after(i))
        return carry

    lax.fori_loop(0, n // nb, step, 0)
    store = pltpu.make_async_copy(o_ref, inverse_hbm, sem.at[1])
    store.start()
    store.wait()


def invert_factor(block):
    n = block.shape[0]
    anywhere = pl.BlockSpec(memory_space=pl.ANY)
    return pl.pallas_call(
        invert_kernel,
        out_shape=jax.ShapeDtypeStruct((n, n), jnp.float32),
        in_specs=[anywhere],
        out_specs=anywhere,
        scratch_shapes=[
            pltpu.VMEM((n, n), jnp.float32),
            pltpu.VMEM((128, 128), jnp.float32),
            pltpu.VMEM((128, 128), jnp.float32),
            pltpu.VMEM((n, n), jnp.float32),
            pltpu.SemaphoreType.DMA((2,)),
        ],
        compiler_params=pltpu.CompilerParams(vmem_limit_bytes=16 * 2**20),
        cost_estimate=pl.CostEstimate(flops=10**10, bytes_accessed=2 * 10**6, transcendentals=0),
        name="invert_factor",
    )(block)


def pack_kernel(panel_hbm, truth_hbm, packed_hbm, panel, truth, packed, sem):
    first = pltpu.make_async_copy(panel_hbm, panel, sem.at[0])
    second = pltpu.make_async_copy(truth_hbm, truth, sem.at[1])
    first.start()
    second.start()
    second.wait()
    packed[28:32, :] = jnp.zeros((4, 512), jnp.float32)
    for q in range(4):
        packed[28:32, 128 * q:128 * q + 64] = truth[4 * q:4 * q + 4, 256:320]
    packed[32:40, 0:256] = truth[0:8, 0:256]
    packed[32:40, 256:512] = truth[8:16, 0:256]
    first.wait()
    packed[0:28, :] = panel[...]
    store = pltpu.make_async_copy(packed, packed_hbm, sem.at[2])
    store.start()
    store.wait()


def pack(panel, truth):
    f32 = jnp.float32
    hbm = pl.BlockSpec(memory_space=pltpu.HBM)
    keep = pltpu.with_memory_space_constraint
    return pl.pallas_call(
        pack_kernel,
        out_shape=jax.ShapeDtypeStruct((40, 512), f32),
        in_specs=[hbm, hbm],
        out_specs=hbm,
        scratch_shapes=[
            pltpu.VMEM((28, 512), f32),
            pltpu.VMEM((16, 320), f32),
            pltpu.VMEM((40, 512), f32),
            pltpu.SemaphoreType.DMA((3,)),
        ],
        compiler_params=pltpu.CompilerParams(vmem_limit_bytes=2 * 2**20),
        name="pack",
    )(keep(panel, pltpu.HBM), keep(truth, pltpu.HBM))


def copy_kernel(strip_ref, copies_hbm, sem):
    copies = [pltpu.make_async_copy(strip_ref, copies_hbm.at[i], sem.at[i]) for i in range(16)]
    for copy in copies:
        copy.start()
    for copy in copies:
        copy.wait()


def copy_out(strip):
    return pl.pallas_call(
        copy_kernel,
        out_shape=jax.ShapeDtypeStruct((16,) + strip.shape, strip.dtype),
        in_specs=[pl.BlockSpec(memory_space=pltpu.VMEM)],
        out_specs=pl.BlockSpec(memory_space=pl.ANY),
        scratch_shapes=[pltpu.SemaphoreType.DMA((16,))],
        compiler_params=pltpu.CompilerParams(vmem_limit_bytes=4 * 2**20),
        name="copy_out",
    )(strip)


def thrice(a, b, dims):
    dot = lambda p, q: lax.dot_general(p, q, dims, preferred_element_type=jnp.float32)
    return dot(a[0], b[0]) + dot(a[0], b[1]) + dot(a[1], b[0])


def dealt_kernel(inverse_any, dealt_any, panel_hbm, w_high, w_low, factor_hbm, inverse, dealt, stack, factor, sem):
    loads = [
        pltpu.make_async_copy(src, dst, sem.at[i])
        for i, (src, dst) in enumerate([(dealt_any, dealt), (panel_hbm, factor), (inverse_any, inverse)])
    ]
    for load in loads:
        load.start()
    loads[0].wait()
    loads[1].wait()
    for r in range(16):
        stack[28 * r:28 * r + 28, :] = dealt[r]
    stack[448:476, :] = factor[...]
    stack[476:480, :] = jnp.zeros((4, 512), jnp.float32)
    loads[2].wait()
    dot = lambda p, q, dims: lax.dot_general(p, q, dims, precision=HI, preferred_element_type=jnp.float32)
    left = dot(stack[:, :256], inverse[:256, :256], NT)
    right = dot(stack[...], inverse[256:, :], NT)
    factor[:, :256] = left[448:476, :]
    factor[:, 256:] = right[448:476, :]
    w_left = dot(left[:448], inverse[:256, :256], NN) + dot(right[:448], inverse[256:, :256], NN)
    w_right = dot(right[:448], inverse[256:, 256:], NN)
    w_high[:, :256], w_low[:, :256] = halves(w_left)
    w_high[:, 256:], w_low[:, 256:] = halves(w_right)
    store = pltpu.make_async_copy(factor, factor_hbm, sem.at[3])
    store.start()
    store.wait()


def solve_dealt(inverse, dealt, panel):
    f32, bf16 = jnp.float32, jnp.bfloat16
    anywhere, hbm = pl.BlockSpec(memory_space=pl.ANY), pl.BlockSpec(memory_space=pltpu.HBM)
    half = pltpu.VMEM((448, 512), bf16)
    vmem = pl.BlockSpec(memory_space=pltpu.VMEM)
    return pl.pallas_call(
        dealt_kernel,
        out_shape=(half, half, jax.ShapeDtypeStruct((28, 512), f32)),
        in_specs=[anywhere] * 2 + [hbm],
        out_specs=(vmem, vmem, hbm),
        scratch_shapes=[
            pltpu.VMEM((512, 512), f32),
            pltpu.VMEM((16, 28, 512), f32),
            pltpu.VMEM((480, 512), f32),
            pltpu.VMEM((28, 512), f32),
            pltpu.SemaphoreType.DMA((4,)),
        ],
        compiler_params=pltpu.CompilerParams(vmem_limit_bytes=16 * 2**20),
        cost_estimate=pl.CostEstimate(flops=10**9, bytes_accessed=2 * 10**6, transcendentals=0),
        name="solve_dealt",
    )(inverse, dealt, pltpu.with_memory_space_constraint(panel, pltpu.HBM))


def apply_kernel(
    col_ref, inverse_any, w_high, w_low, gathered_hbm, trailing_hbm, rest_hbm,
    updated_hbm, solved_hbm, truth_hbm,
    own, gathered, trailing, rest, stack, truth, solved, sem, out_sem,
):
    at = pl.ds(pl.multiple_of(col_ref[0] * 16, 16), 16)
    pieces = ((0, 10), (10, 19), (19, 28), (28, 32))
    loads = [
        pltpu.make_async_copy(src, dst, sem.at[i])
        for i, (src, dst) in enumerate(
            [(gathered_hbm.at[a:b], gathered.at[a:b]) for a, b in pieces]
            + [
                (trailing_hbm, trailing),
                (inverse_any.at[at], own), (rest_hbm, rest),
            ]
        )
    ]
    stores = []

    def unpack(first, last):
        for c in range(first, last):
            stack[28 * c:28 * c + 28, :] = gathered[c, 0:28, :]
            truth[16 * c:16 * c + 8, 0:256] = gathered[c, 32:40, 0:256]
            truth[16 * c + 8:16 * c + 16, 0:256] = gathered[c, 32:40, 256:512]
            for q in range(4):
                truth[16 * c + 4 * q:16 * c + 4 * q + 4, 256:384] = gathered[c, 28:32, 128 * q:128 * q + 128]

    def put(src, dst):
        store = pltpu.make_async_copy(src, dst, out_sem.at[len(stores)])
        store.start()
        stores.append(store)

    def product(first, last):
        high, low = halves(stack[first:last, :])
        dot = lambda p, q: lax.dot_general(p, q, NT, preferred_element_type=jnp.float32)
        both = dot(jnp.concatenate([w_high[...], w_low[...]], 0), high)
        return both[:448] + both[448:] + dot(w_high[...], low)

    def finish(first, last, value):
        trailing[:, first:last] = trailing[:, first:last] - value

    def send(first, last):
        put(trailing.at[:, first:last], updated_hbm.at[:, first:last])

    for i in (0, 1):
        loads[i].start()
    loads[0].wait()
    for i in (2, 3, 4, 6, 5):
        loads[i].start()
    unpack(0, 10)
    loads[1].wait()
    value = product(0, 256)
    unpack(10, 19)
    for i in (2, 3):
        loads[i].wait()
    later = product(256, 512)
    unpack(19, 32)
    columns = halves(truth[...].T[0:320, :])
    for i in (4, 6, 5):
        loads[i].wait()
    finish(0, 256, value)
    finish(256, 512, later)
    value = product(512, 768)
    send(0, 256)
    send(256, 512)
    finish(512, 768, value)
    rest[...] = rest[...] - thrice(columns, (w_high[...], w_low[...]), NT)
    solved[...] = thrice(halves(own[...]), columns, NT)
    value = product(768, 896)
    send(512, 768)
    put(rest, truth_hbm)
    put(solved, solved_hbm)
    finish(768, 896, value)
    send(768, 896)
    for store in stores:
        store.wait()


def apply_inverse(column, inverse, w_high, w_low, gathered, trailing, rest):
    f32, bf16 = jnp.float32, jnp.bfloat16
    anywhere, hbm = pl.BlockSpec(memory_space=pl.ANY), pl.BlockSpec(memory_space=pltpu.HBM)
    keep = pltpu.with_memory_space_constraint
    return pl.pallas_call(
        apply_kernel,
        out_shape=(
            jax.ShapeDtypeStruct((448, 896), f32),
            jax.ShapeDtypeStruct((16, 320), f32),
            jax.ShapeDtypeStruct((320, 448), f32),
        ),
        in_specs=[pl.BlockSpec(memory_space=pltpu.SMEM), anywhere] + [pl.BlockSpec(memory_space=pltpu.VMEM)] * 2 + [hbm] * 3,
        out_specs=(hbm,) * 3,
        scratch_shapes=[
            pltpu.VMEM((16, 512), f32),
            pltpu.VMEM((32, 40, 512), f32),
            pltpu.VMEM((448, 896), f32),
            pltpu.VMEM((320, 448), f32),
            pltpu.VMEM((896, 512), f32),
            pltpu.VMEM((512, 384), f32),
            pltpu.VMEM((16, 320), f32),
            pltpu.SemaphoreType.DMA((7,)),
            pltpu.SemaphoreType.DMA((6,)),
        ],
        compiler_params=pltpu.CompilerParams(vmem_limit_bytes=24 * 2**20),
        cost_estimate=pl.CostEstimate(flops=4 * 10**9, bytes_accessed=10**7, transcendentals=0),
        name="apply_inverse",
    )(column, inverse, keep(w_high, pltpu.VMEM), keep(w_low, pltpu.VMEM), *(keep(x, pltpu.HBM) for x in (gathered, trailing, rest)))


def per_device(diag_block, panel, trailing, truth_panel, truth_rest):
    rows, columns = ("x", "y"), ("z", "k")
    packed = pack(panel, truth_panel.T)
    gathered = lax.all_gather(packed, columns, axis=0, tiled=False)
    small = jnp.broadcast_to(diag_block.reshape(1, 4, 128), (32, 4, 128))
    pieces = lax.all_to_all(small, columns, 0, 0)
    strip = pieces.reshape(32, 4, 8, 16).transpose(1, 2, 0, 3).reshape(32, 512)
    whole = lax.all_to_all(copy_out(strip), rows, 0, 0).reshape(512, 512)
    copies, whole = lax.optimization_barrier((copy_out(panel), whole))
    dealt = lax.all_to_all(copies, rows, 0, 0)
    inverse = invert_factor(whole)
    column = (lax.axis_index("z") * 2 + lax.axis_index("k")).astype(jnp.int32)[None]
    w_high, w_low, factor = solve_dealt(inverse, dealt, panel)
    updated, solved, truth_updated = apply_inverse(
        column, inverse, w_high, w_low, gathered, trailing.T, truth_rest
    )
    return factor, updated.T, solved.T, truth_updated


def solution(mesh):
    fine = jax.sharding.Mesh(mesh.devices.reshape(4, 4, 16, 2), ("x", "y", "z", "k"))
    rows, columns = ("x", "y"), ("z", "k")
    tiled, whole = P(rows, columns), P(rows + columns, None)
    return jax.shard_map(
        per_device,
        mesh=fine,
        in_specs=(tiled, whole, tiled, tiled, tiled),
        out_specs=(whole, tiled, tiled, tiled),
        check_vma=False,
    )
```
